512 devices in a mesh: event: 2 (over core), dom: 256 (over z, y, x).
Axes of the slice: x: 4, y: 8, z: 8, core: 2. Of those that a mesh axis runs over, the one named last changes fastest.
Arguments:
- kernels: bfloat16 [4, 256, 64, 125, 128], P('event', 'dom'), may hold values from -12 to 12
- counts: int32 [4, 256, 64, 128], P('event', 'dom'), may hold values from 0 to 3
- volume: bfloat16 [256, 64, 128], P('dom', 'event'), may hold values from 0.29882812 to 3
- tables: bfloat16 [32, 128, 128], replicated, may hold values from 0.049804688 to 1
- pair_offset: int32 [256, 2, 32, 16], P('dom', 'event'), may hold values from 0 to 64, as said below
- pair_table: int32 [256, 2, 32, 16], P('dom', 'event'), may hold values from 0 to 31
Outputs:
- smoothed: bfloat16 [256, 64, 125, 128], P('dom', 'event')
The draws below stay inside these ranges and needn't reach their ends.
Inputs may be any that keep to these rules, and one draw needn't show every extreme that they name: `pair_offset`: for each block of a device the 16 offsets are distinct and the first is 32.
All inputs are finite; a program needn't handle non-finite values.
Results may differ from the reference program's by a relative error of at most 0.0075.
Values may be sent and summed in bfloat16 or wider, within the bound.
No kernel may reach another device: no remote copies, remote signals or barrier semaphores. Data moves between devices by JAX's collectives and lax.ppermute only.
A program may use at most 64 MiB of HBM per device.

```python
import math
import jax
import jax.numpy as jnp
from jax import lax

G = 125
BLK = 128
EV_DEV = 2
OWN_BLK = 32
PB = 16
TABLES = 32
EVENTS = 4
NSUB = 2
PART_BLK = 64
NPART = 256
N_EVENT = 2


def draw_kernels(key, part):
    first, second = jax.random.split(key)
    shape = (EVENTS, NPART, PART_BLK, G, BLK)
    level_shape = (EVENTS, NPART, PART_BLK, G, 1)
    rough = jax.random.normal(first, shape, jnp.float32)
    level = jax.random.normal(second, level_shape, jnp.float32)
    return jnp.clip(rough + level, -12.0, 12.0).astype(jnp.bfloat16)


def draw_pair_offset(key, part):
    window = 2 * OWN_BLK + 1
    scores = jax.random.randint(key, (NPART, NSUB, OWN_BLK, window), 0, 2 ** 20) * 1024
    columns = jnp.arange(window, dtype=jnp.int32)
    scores = scores + columns
    scores = jnp.where(columns == OWN_BLK, -1, scores)
    order = jnp.argsort(scores, axis=-1)
    return order[..., :PB].astype(jnp.int32)


def touch_ends(drawn, rng, low, high):
    longest = drawn.shape.index(max(drawn.shape))
    spots = []
    for shift in (0, 1):
        where = [jax.random.randint(jax.random.fold_in(rng, axis), (), 0, length) for axis, length in enumerate(drawn.shape)]
        where[longest] = (where[longest] + shift) % drawn.shape[longest]
        spots.append(tuple(where))
    return drawn.at[spots[0]].set(low).at[spots[1]].set(high)


def level_of(stream_key, dims, cuts, smallest, top_value):
    loudness = 1.0
    for dim, blocks in cuts:
        heights = jax.random.uniform(jax.random.fold_in(jax.random.fold_in(stream_key, 6), dim), (blocks,), jnp.float32, smallest / len(cuts), top_value / len(cuts))
        loudness = loudness * jnp.repeat(jnp.exp(heights), dims[dim] // blocks).reshape((-1,) + (1,) * (len(dims) - 1 - dim))
    return loudness


def setup_inputs(seed: int = 0) -> dict:
    key_list = jax.random.split(jax.random.key(seed), 7)
    kernels = draw_kernels(jax.random.fold_in(key_list[6], 71), 0)
    counts = touch_ends(jax.random.randint(key_list[1], (EVENTS, NPART, PART_BLK, BLK), 0, 4), jax.random.fold_in(key_list[1], 1), 0, 3).astype(jnp.int32)
    volume = jnp.clip(jnp.exp(math.log(3.0) - 2.306499 * jax.random.uniform(key_list[2], (NPART, PART_BLK, BLK), jnp.float32) ** level_of(key_list[2], (NPART, PART_BLK, BLK), ((0, 256), (1, 2)), -0.2, 0.2)), 0.29882812, 3.0).astype(jnp.bfloat16)
    tables = jnp.clip(jax.random.uniform(key_list[3], (TABLES, BLK, BLK), jnp.float32, 0.049804688, 1.0), 0.049804688, 1.0).astype(jnp.bfloat16)
    pair_offset = draw_pair_offset(jax.random.fold_in(key_list[6], 71), 0)
    pair_table = touch_ends(jax.random.randint(key_list[5], (NPART, NSUB, OWN_BLK, PB), 0, TABLES), jax.random.fold_in(key_list[5], 1), 0, TABLES - 1).astype(jnp.int32)
    return dict(kernels=kernels, counts=counts, volume=volume, tables=tables, pair_offset=pair_offset, pair_table=pair_table)


def add_terms(extended, targets, contrib):
    return extended.at[targets].add(contrib)

def contributions(source, offsets, table_ids, tables):
    extended = jnp.zeros((NSUB, 3 * OWN_BLK, G + 1, BLK), jnp.float32)
    places = jnp.arange(OWN_BLK, dtype=jnp.int32)
    for which in range(PB):
        matrices = tables[table_ids[:, :, which]].astype(jnp.float32)
        contrib = jnp.einsum('sbgc,sbct->sbgt', source, matrices, precision=lax.Precision.HIGHEST)
        targets = (places[None, :] + offsets[:, :, which]).astype(jnp.int32)
        extended = jax.vmap(add_terms)(extended, targets, contrib)
    return extended

def reference(kernels, counts, volume, tables, pair_offset, pair_table):

    def per_partition(index):
        block = lax.dynamic_index_in_dim(kernels, index, 1, keepdims=False)
        grouped = block.reshape(N_EVENT, EV_DEV, PART_BLK, G, BLK)
        partial_value = lax.optimization_barrier(jnp.sum(grouped.astype(jnp.float32), axis=1)).astype(jnp.bfloat16)
        summed = lax.optimization_barrier(jnp.sum(partial_value.astype(jnp.float32), axis=0))
        count_part = lax.dynamic_index_in_dim(counts, index, 1, keepdims=False)
        hits = lax.optimization_barrier(jnp.sum(count_part.astype(jnp.float32), axis=0))
        vol_part = lax.dynamic_index_in_dim(volume, index, 0, keepdims=False)
        weighted = (summed * vol_part.astype(jnp.float32)[:, None, :] / jnp.sqrt(1.0 + hits)[:, None, :]).astype(jnp.bfloat16)
        source = jnp.concatenate([weighted, vol_part[:, None, :]], axis=1).astype(jnp.float32)
        source = source.reshape(NSUB, OWN_BLK, G + 1, BLK)
        offsets = lax.dynamic_index_in_dim(pair_offset, index, 0, keepdims=False)
        table_ids = lax.dynamic_index_in_dim(pair_table, index, 0, keepdims=False)
        return contributions(source, offsets, table_ids, tables)
    extended = lax.map(per_partition, jnp.arange(NPART, dtype=jnp.int32))
    middle = extended[:, :, OWN_BLK:2 * OWN_BLK]
    empty = jnp.zeros((1, NSUB, OWN_BLK, G + 1, BLK), jnp.float32)
    from_next = jnp.concatenate([extended[1:, :, :OWN_BLK], empty], axis=0)
    from_prev = jnp.concatenate([empty, extended[:-1, :, 2 * OWN_BLK:]], axis=0)
    accumulated = (middle + from_next + from_prev).reshape(NPART, PART_BLK, G + 1, BLK)
    result = accumulated[:, :, :G, :] / accumulated[:, :, G:G + 1, :]
    return result.astype(jnp.bfloat16)
```

```python
import functools

import jax
import jax.numpy as jnp
from jax import lax
from jax.experimental import pallas as pl
from jax.experimental.pallas import tpu as pltpu
from jax.sharding import PartitionSpec as P


OWN = 32
G = 125
ROWS = 128
W = 128
PB = 16
CH = 8
NCH = OWN // CH
U = 4
LIST = 640
DUMMY = OWN << 16
COPY_ALIASED = False
MIB = 1 << 20


HBM = pl.BlockSpec(memory_space=pltpu.HBM)
VMEM = pl.BlockSpec(memory_space=pltpu.VMEM)
SMEM = pl.BlockSpec(memory_space=pltpu.SMEM)


def on_chip(shape, dtype):
    return pltpu.VMEM(shape, dtype)


def in_vmem(x):
    return pltpu.with_memory_space_constraint(x, pltpu.VMEM)


def in_hbm(x):
    return pltpu.with_memory_space_constraint(x, pltpu.HBM)


def params(mib):
    return pltpu.CompilerParams(vmem_limit_bytes=mib * MIB)


def cost(flops, nbytes):
    return pl.CostEstimate(flops=flops, bytes_accessed=nbytes, transcendentals=0)


def shifted(value, axis, steps):
    count = lax.axis_size(axis)
    first, last = (max(0, -steps), min(count, count - steps))
    return lax.ppermute(value, axis, [(source, source + steps) for source in range(first, last)])


OUTER = ((0, 0), (24, 8))
INNER = ((8, 0), (16, 8))


def fetch(kern, buf, sems, base, pieces):
    copies = [
        pltpu.make_async_copy(
            kern.at[:, 0, :, pl.ds(base + first, CH)],
            buf.at[:, :, pl.ds(place, CH)],
            sems.at[n],
        )
        for n, (first, place) in enumerate(pieces)
    ]
    for copy in copies:
        copy.start()
    return copies


def two_events(buf, place, out):
    total = buf[0, :, place : place + CH].astype(jnp.float32)
    total = total + buf[1, :, place : place + CH].astype(jnp.float32)
    out[0:G, place : place + CH] = total.astype(jnp.bfloat16)


def put_counts(cbuf, pieces, out):
    for first, place in pieces:
        total = cbuf[0, first : first + CH] + cbuf[1, first : first + CH]
        out[G, place : place + CH] = total.astype(jnp.float32).astype(jnp.bfloat16)


def send_outer_kernel(kern, counts, out, buf, cbuf, sems, csem):
    base = (1 - lax.axis_index("event")) * OWN
    copies = fetch(kern, buf, sems, base, OUTER)
    ccopy = pltpu.make_async_copy(counts.at[:, 0, pl.ds(base, OWN)], cbuf, csem)
    ccopy.start()
    for copy, (_, place) in zip(copies, OUTER):
        copy.wait()
        two_events(buf, place, out)
    ccopy.wait()
    put_counts(cbuf, OUTER, out)


def send_inner_kernel(
    kern, counts, off, tab, out, own_outer, own_inner, own_l, prev_l, next_l,
    buf, cbuf, sems, csem,
):
    me = lax.axis_index("event")
    other = 1 - me
    outer = fetch(kern, buf.at[0], sems.at[0], me * OWN, OUTER)
    others = fetch(kern, buf.at[1], sems.at[1], other * OWN, INNER)
    inner = fetch(kern, buf.at[2], sems.at[2], me * OWN, INNER)
    ccopies = [
        pltpu.make_async_copy(counts.at[:, 0, pl.ds(side * OWN, OWN)], cbuf.at[n], csem.at[n])
        for n, side in enumerate((me, other))
    ]
    for copy in ccopies:
        copy.start()

    first = 8
    lists = (prev_l, own_l, next_l)
    for ref in lists:
        ref[0] = first
    fill = (jnp.int32(first),) * 3
    for c in range(NCH):

        def block(j, fill):
            b = c * CH + j
            prev_n, own_n, next_n = fill
            for k in range(PB):
                x = b + off[0, 0, k, b]
                code = j | (tab[0, 0, k, b] << 8) | ((x & (OWN - 1)) << 16)
                for ref, n in zip(lists, (prev_n, own_n, next_n)):
                    ref[n] = code
                part = x >> 5
                prev_n = prev_n + (part == 0).astype(jnp.int32)
                own_n = own_n + (part == 1).astype(jnp.int32)
                next_n = next_n + (part == 2).astype(jnp.int32)
            return prev_n, own_n, next_n

        fill = lax.fori_loop(0, CH, block, fill)
        padded = []
        for ref, n in zip(lists, fill):
            for u in range(U - 1):
                ref[n + u] = DUMMY
            n = (n + (U - 1)) & ~(U - 1)
            ref[c + 1] = n
            padded.append(n)
        fill = tuple(padded)

    for copy in ccopies:
        copy.wait()
    for which, (copies, pieces, dst, side) in enumerate(
        ((outer, OUTER, own_outer, 0), (others, INNER, out, 1), (inner, INNER, own_inner, 0))
    ):
        for copy, (_, place) in zip(copies, pieces):
            copy.wait()
            two_events(buf.at[which], place, dst)
        put_counts(cbuf.at[side], pieces, dst)


def source_kernel(pieces, own, got, vol, low, high):
    for (first, place), dst in zip(pieces, (low, high)):
        span = slice(place, place + CH)
        v = vol[0, first : first + CH]
        hits = own[G, span].astype(jnp.float32) + got[G, span].astype(jnp.float32)
        factor = v.astype(jnp.float32) / jnp.sqrt(1.0 + hits)
        total = own[0:G, span].astype(jnp.float32) + got[0:G, span].astype(jnp.float32)
        dst[0:G] = (total * factor[None]).astype(jnp.bfloat16)
        dst[G] = v


def by_block(source, dst):
    x = source[...].astype(jnp.float32)
    x = jnp.concatenate([x, jnp.zeros((ROWS - G - 1, CH, W), jnp.float32)], axis=0)
    dst[...] = jnp.transpose(x, (1, 0, 2)).astype(jnp.bfloat16)


def add_terms(lst, c, source, tables, acc):
    start = lst[c]
    steps = (lst[c + 1] - start) >> 2

    def step(i, carry):
        at = start + i * U
        for u in range(U):
            code = lst[at + u]
            term = jnp.dot(
                source[code & (CH - 1)],
                tables[(code >> 8) & 31],
                preferred_element_type=jnp.float32,
            )
            x = code >> 16
            acc[x] = acc[x] + term
        return carry

    lax.fori_loop(0, steps, step, 0)


def own_kernel(lst, s0, s1, s2, s3, tables, acc, mats):
    def clear(i, carry):
        acc[i] = jnp.zeros((ROWS, W), jnp.float32)
        return carry

    lax.fori_loop(0, OWN + 1, clear, 0)
    for c, source in enumerate((s0, s1, s2, s3)):
        by_block(source, mats.at[c])
        add_terms(lst, c, mats.at[c], tables, acc)


def received_terms(step, next_l, prev_l, from_next, from_prev, tables, acc, mats):
    by_block(from_next, mats.at[0])
    by_block(from_prev, mats.at[1])
    add_terms(next_l, step, mats.at[0], tables, acc)
    add_terms(prev_l, NCH - 1 - step, mats.at[1], tables, acc)


def chunk_kernel(step, next_l, prev_l, from_next, from_prev, tables, acc_in, acc, mats):
    if COPY_ALIASED:
        acc[...] = acc_in[...]
    received_terms(step, next_l, prev_l, from_next, from_prev, tables, acc, mats)


def last_kernel(next_l, prev_l, from_next, from_prev, tables, acc_in, out, acc, mats, stage, sem):
    if COPY_ALIASED:
        acc[...] = acc_in[...]
    received_terms(NCH - 1, next_l, prev_l, from_next, from_prev, tables, acc, mats)
    for c in range(NCH):
        span = slice(c * CH, c * CH + CH)
        scale = 1.0 / acc[span, G : G + 1]
        result = jnp.transpose(acc[span] * scale, (1, 0, 2))
        stage[:, span] = result[0:G].astype(jnp.bfloat16)
    copy = pltpu.make_async_copy(stage, out.at[0], sem)
    copy.start()
    copy.wait()


def per_device(kernels, counts, volume, tables, pair_offset, pair_table):
    bf16, f32, i32 = jnp.bfloat16, jnp.float32, jnp.int32
    dma = pltpu.SemaphoreType.DMA
    half = 2 * CH
    kernels = in_hbm(jnp.transpose(kernels, (0, 1, 3, 2, 4)))
    pair_offset = jnp.transpose(pair_offset, (0, 1, 3, 2))
    pair_table = jnp.transpose(pair_table, (0, 1, 3, 2))
    swap = [(0, 1), (1, 0)]

    to_outer = pl.pallas_call(
        send_outer_kernel,
        out_shape=on_chip((G + 1, half, W), bf16),
        in_specs=[HBM, HBM],
        out_specs=VMEM,
        scratch_shapes=[
            pltpu.VMEM((2, G, half, W), bf16),
            pltpu.VMEM((2, OWN, W), i32),
            dma((2,)),
            dma,
        ],
        compiler_params=params(8),
        cost_estimate=cost(1 << 20, 1 << 20),
        name="send_outer",
    )(kernels, counts)
    got_outer = lax.ppermute(to_outer, "event", swap)

    to_inner, own_outer, own_inner, own_l, prev_l, next_l = pl.pallas_call(
        send_inner_kernel,
        out_shape=[on_chip((G + 1, half, W), bf16)] * 3
        + [jax.ShapeDtypeStruct((LIST,), i32)] * 3,
        in_specs=[HBM, HBM, SMEM, SMEM],
        out_specs=[VMEM] * 3 + [SMEM] * 3,
        scratch_shapes=[
            pltpu.VMEM((3, 2, G, half, W), bf16),
            pltpu.VMEM((2, 2, OWN, W), i32),
            dma((3, 2)),
            dma((2,)),
        ],
        compiler_params=params(8),
        cost_estimate=cost(1 << 20, 6 << 20),
        name="send_inner",
    )(kernels, counts, pair_offset, pair_table)
    got_inner = lax.ppermute(to_inner, "event", swap)

    def source(pieces, own, got):
        return pl.pallas_call(
            functools.partial(source_kernel, pieces),
            out_shape=[on_chip((G + 1, CH, W), bf16)] * 2,
            in_specs=[VMEM] * 3,
            out_specs=[VMEM] * 2,
            compiler_params=params(4),
            cost_estimate=cost(1 << 20, 1 << 20),
        )(own, in_vmem(got), volume)

    def moved(value, steps):
        return shifted(value, "dom", steps)

    s0, s3 = source(OUTER, own_outer, got_outer)
    next_0 = moved(s0, -1)
    prev_0 = moved(s3, 1)
    s1, s2 = source(INNER, own_inner, got_inner)
    lists_next = moved(prev_l, -1)
    lists_prev = moved(next_l, 1)
    from_next = [next_0] + [moved(s, -1) for s in (s1, s2, s3)]
    from_prev = [prev_0] + [moved(s, 1) for s in (s2, s1, s0)]

    acc_shape = on_chip((OWN + 1, ROWS, W), f32)
    term = 2 * ROWS * W * W
    acc = pl.pallas_call(
        own_kernel,
        out_shape=acc_shape,
        in_specs=[SMEM] + [VMEM] * 5,
        out_specs=VMEM,
        scratch_shapes=[pltpu.VMEM((NCH, CH, ROWS, W), bf16)],
        compiler_params=params(4),
        cost_estimate=cost(256 * term, 16 << 20),
        name="own_terms",
    )(own_l, s0, s1, s2, s3, tables)
    mats = pltpu.VMEM((2, CH, ROWS, W), bf16)
    for step in range(NCH - 1):
        acc = pl.pallas_call(
            functools.partial(chunk_kernel, step),
            out_shape=acc_shape,
            in_specs=[SMEM, SMEM] + [VMEM] * 4,
            out_specs=VMEM,
            scratch_shapes=[mats],
            input_output_aliases={5: 0},
            compiler_params=params(4),
            cost_estimate=cost(64 * term, 4 << 20),
        )(lists_next, lists_prev, in_vmem(from_next[step]), in_vmem(from_prev[step]), tables, acc)
    out, _ = pl.pallas_call(
        last_kernel,
        out_shape=[jax.ShapeDtypeStruct((1, G, OWN, W), bf16), acc_shape],
        in_specs=[SMEM, SMEM] + [VMEM] * 4,
        out_specs=[HBM, VMEM],
        input_output_aliases={5: 1},
        scratch_shapes=[mats, pltpu.VMEM((G, OWN, W), bf16), dma],
        compiler_params=params(4),
        cost_estimate=cost(16 * term, 4 << 20),
        name="terms_last",
    )(lists_next, lists_prev, in_vmem(from_next[-1]), in_vmem(from_prev[-1]), tables, acc)
    return jnp.transpose(out, (0, 2, 1, 3))


def solution(mesh):
    in_specs = (
        P("event", "dom", None, None, None),
        P("event", "dom", None, None),
        P("dom", "event", None),
        P(),
        P("dom", "event", None, None),
        P("dom", "event", None, None),
    )
    return jax.shard_map(
        per_device,
        mesh=mesh,
        in_specs=in_specs,
        out_specs=P("dom", "event", None, None),
        check_vma=False,
    )
```

```python
import jax
import jax.numpy as jnp
from jax import lax
from jax.experimental import pallas as pl
from jax.experimental.pallas import tpu as pltpu
from jax.sharding import PartitionSpec as P


OWN = 32
HALF = OWN // 2
G = 125
ADJ = G + 1
ROWS = 128
W = 128
PB = 16
K = 4
T = 4
LIST = OWN + 8
OWN_LANE = 2 * OWN
MIB = 1 << 20
COPY_ALIASED = False


HBM = pl.BlockSpec(memory_space=pltpu.HBM)
VMEM = pl.BlockSpec(memory_space=pltpu.VMEM)
SMEM = pl.BlockSpec(memory_space=pltpu.SMEM)


def on_chip(shape, dtype):
    return pltpu.VMEM(shape, dtype)


def in_vmem(x):
    return pltpu.with_memory_space_constraint(x, pltpu.VMEM)


def in_hbm(x):
    return pltpu.with_memory_space_constraint(x, pltpu.HBM)


def params(mib):
    return pltpu.CompilerParams(vmem_limit_bytes=mib * MIB)


def cost(flops, nbytes):
    return pl.CostEstimate(flops=flops, bytes_accessed=nbytes, transcendentals=0)


def partial_sums(kern, counts, base, out, buf, cbuf, sems, csem):
    copies = []
    for n in range(2):
        copies.append(
            pltpu.make_async_copy(
                kern.at[:, 0, :, pl.ds(base + n * HALF, HALF)],
                buf.at[:, :, pl.ds(n * HALF, HALF)],
                sems.at[n],
            )
        )
    ccopy = pltpu.make_async_copy(counts.at[:, 0, pl.ds(base, OWN)], cbuf, csem)
    for copy in copies + [ccopy]:
        copy.start()
    yield
    ccopy.wait()
    out[G] = (cbuf[0] + cbuf[1]).astype(jnp.float32).astype(jnp.bfloat16)
    for n, copy in enumerate(copies):
        copy.wait()
        span = slice(n * HALF, (n + 1) * HALF)
        total = buf[0, :, span].astype(jnp.float32) + buf[1, :, span].astype(jnp.float32)
        out[0:G, span] = total.astype(jnp.bfloat16)


def send_kernel(kern, counts, out, *scratch):
    base = (1 - lax.axis_index("event")) * OWN
    for _ in partial_sums(kern, counts, base, out, *scratch):
        pass


def keep_kernel(kern, counts, off, tab, out, adj, *scratch):
    steps = partial_sums(kern, counts, lax.axis_index("event") * OWN, out, *scratch)
    next(steps)
    odd = lax.rem(lax.axis_index("dom"), 2)
    b = lax.broadcasted_iota(jnp.int32, (PB, OWN), 1)
    x = off[0, 0] + b
    part = x >> 5
    group = jnp.where(part == 1, 2, jnp.where(part == 0, odd, 1 - odd))
    lane = (x & (OWN - 1)) + group * OWN
    value = (tab[0, 0] + 1).astype(jnp.float32)
    spot = lax.broadcasted_iota(jnp.int32, (3 * OWN, OWN), 0)
    turned = jnp.zeros((3 * OWN, OWN), jnp.float32)
    for k in range(PB):
        turned = turned + jnp.where(spot == lane[k : k + 1], value[k : k + 1], 0.0)
    wide = jnp.concatenate([turned, jnp.zeros((OWN, OWN), jnp.float32)], axis=0)
    wide = jnp.concatenate([wide, jnp.zeros((W, W - OWN), jnp.float32)], axis=1)
    adj[...] = jnp.transpose(wide, (1, 0))[0:OWN]
    for _ in steps:
        pass


def source_kernel(own, got, vol, adj, first, second):
    odd = lax.rem(lax.axis_index("dom"), 2)
    for dst, half in ((first, odd), (second, 1 - odd)):
        span = pl.ds(pl.multiple_of(half * HALF, HALF), HALF)
        v = vol[0, span].astype(jnp.float32)
        hits = own[G, span].astype(jnp.float32) + got[G, span].astype(jnp.float32)
        factor = v / jnp.sqrt(1.0 + hits)
        total = own[0:G, span].astype(jnp.float32) + got[0:G, span].astype(jnp.float32)
        rows = [total * factor[None], v[None], adj[span][None]]
        rows.append(jnp.zeros((ROWS - ADJ - 1, HALF, W), jnp.float32))
        block = jnp.concatenate(rows, axis=0)
        dst[...] = jnp.transpose(block, (1, 0, 2)).astype(jnp.bfloat16)


def make_lists(p, q, p_lane, q_lane, lanes, codes, sem):
    adj = []
    for ref, lane in ((p, p_lane), (q, q_lane)):
        a = ref[:, ADJ].astype(jnp.float32)
        adj.append(pltpu.roll(a, (W - lane) % W, 1) if lane else a)
    adj = jnp.concatenate(adj, axis=0)
    there = adj > 0.5
    ones = jnp.where(there, 1.0, 0.0)
    row = lax.broadcasted_iota(jnp.int32, (OWN, OWN), 0)
    col = lax.broadcasted_iota(jnp.int32, (OWN, OWN), 1)
    below = jnp.where(col < row, 1.0, 0.0)
    rank = jnp.dot(
        below.astype(jnp.bfloat16), ones.astype(jnp.bfloat16), preferred_element_type=jnp.float32
    )
    rank = jnp.where(there, rank, -1.0)
    source = lax.broadcasted_iota(jnp.int32, (OWN, W), 0).astype(jnp.float32)
    code = source + 1.0 + 64.0 * (adj - 1.0)
    for r in range(OWN):
        picked = jnp.sum(jnp.where(rank == float(r), code, 0.0), axis=0, keepdims=True)
        lanes[r : r + 1] = picked.astype(jnp.int32)
    lanes[OWN : OWN + 1] = jnp.sum(ones, axis=0, keepdims=True).astype(jnp.int32)
    copy = pltpu.make_async_copy(lanes, codes, sem)
    copy.start()
    return copy


def term_group(codes, g, x, mats, tables):
    left, right = [], []
    for j in range(K):
        code = codes[g * K + j, x]
        left.append(mats[code & 63])
        right.append(tables[code >> 6])
    return jnp.dot(
        jnp.concatenate(left, axis=1),
        jnp.concatenate(right, axis=0),
        preferred_element_type=jnp.float32,
    )


def add_terms(codes, mats, tables, acc, fresh):
    def targets(t, carry):
        xs = [t * T + u for u in range(T)]
        most = codes[OWN, xs[0]]
        for x in xs[1:]:
            most = jnp.maximum(most, codes[OWN, x])
        if fresh:
            for x in xs:
                acc[x] = term_group(codes, 0, x, mats, tables)

        def group(g, carry):
            for x in xs:
                acc[x] = acc[x] + term_group(codes, g, x, mats, tables)
            return carry

        lax.fori_loop(1 if fresh else 0, (most + (K - 1)) >> 2, group, 0)
        return carry

    lax.fori_loop(0, OWN // T, targets, 0)


def gather_terms(p, q, p_lane, q_lane, tables, acc, mats, lanes, codes, sem, fresh=False):
    copy = make_lists(p, q, p_lane, q_lane, lanes, codes, sem)
    mats[0] = jnp.zeros((ROWS, W), jnp.bfloat16)
    mats[1 : 1 + HALF] = p[...]
    mats[1 + HALF : 1 + OWN] = q[...]
    copy.wait()
    add_terms(codes, mats, tables, acc, fresh)


def own_kernel(first, second, tables, acc, *scratch):
    gather_terms(first, second, OWN_LANE, OWN_LANE, tables, acc, *scratch, fresh=True)


def chunk_kernel(from_b, from_a, tables, acc_in, acc, *scratch):
    if COPY_ALIASED:
        acc[...] = acc_in[...]
    gather_terms(from_b, from_a, 0, OWN, tables, acc, *scratch)


def last_kernel(from_b, from_a, tables, acc_in, out, acc, stage, osem, *scratch):
    if COPY_ALIASED:
        acc[...] = acc_in[...]
    gather_terms(from_b, from_a, 0, OWN, tables, acc, *scratch)
    for c in range(OWN // 8):
        span = slice(c * 8, c * 8 + 8)
        scale = 1.0 / acc[span, G : G + 1]
        result = jnp.transpose(acc[span] * scale, (1, 0, 2))
        stage[:, span] = result[0:G].astype(jnp.bfloat16)
    copy = pltpu.make_async_copy(stage, out.at[0], osem)
    copy.start()
    copy.wait()


def per_device(kernels, counts, volume, tables, pair_offset, pair_table):
    bf16, f32, i32 = jnp.bfloat16, jnp.float32, jnp.int32
    dma = pltpu.SemaphoreType.DMA
    kernels = in_hbm(jnp.transpose(kernels, (0, 1, 3, 2, 4)))
    counts = in_hbm(counts)
    pair_offset = jnp.transpose(pair_offset, (0, 1, 3, 2))
    pair_table = jnp.transpose(pair_table, (0, 1, 3, 2))
    sums = on_chip((G + 1, OWN, W), bf16)
    scratch = [
        pltpu.VMEM((2, G, OWN, W), bf16),
        pltpu.VMEM((2, OWN, W), i32),
        dma((2,)),
        dma,
    ]

    to_other = pl.pallas_call(
        send_kernel,
        out_shape=sums,
        in_specs=[HBM, HBM],
        out_specs=VMEM,
        scratch_shapes=scratch,
        compiler_params=params(6),
        cost_estimate=cost(1 << 20, 4 << 20),
        name="send",
    )(kernels, counts)
    got = lax.ppermute(to_other, "event", [(0, 1), (1, 0)])
    own, adj = pl.pallas_call(
        keep_kernel,
        out_shape=[sums, on_chip((OWN, W), f32)],
        in_specs=[HBM, HBM, VMEM, VMEM],
        out_specs=[VMEM, VMEM],
        scratch_shapes=scratch,
        compiler_params=params(6),
        cost_estimate=cost(1 << 20, 4 << 20),
        name="keep",
    )(kernels, counts, pair_offset, pair_table)
    first, second = pl.pallas_call(
        source_kernel,
        out_shape=[on_chip((HALF, ROWS, W), bf16)] * 2,
        in_specs=[VMEM] * 4,
        out_specs=[VMEM] * 2,
        compiler_params=params(6),
        cost_estimate=cost(1 << 20, 4 << 20),
        name="source",
    )(own, in_vmem(got), volume, adj)

    count = lax.axis_size("dom")

    def swapped(value, start):
        pairs = [(a, a + 1) for a in range(start, count - 1, 2)]
        pairs = pairs + [(b, a) for a, b in pairs]
        return lax.ppermute(value, "dom", pairs)

    b0 = swapped(first, 1)
    a0 = swapped(second, 0)
    b1 = swapped(second, 1)
    a1 = swapped(first, 0)

    acc_shape = on_chip((OWN, ROWS, W), f32)
    term = 2 * ROWS * W * W
    lists = [
        pltpu.VMEM((OWN + 1, ROWS, W), bf16),
        pltpu.VMEM((LIST, W), i32),
        pltpu.SMEM((LIST, W), i32),
        dma,
    ]
    acc = pl.pallas_call(
        own_kernel,
        out_shape=acc_shape,
        in_specs=[VMEM] * 3,
        out_specs=VMEM,
        scratch_shapes=lists,
        compiler_params=params(6),
        cost_estimate=cost(256 * term, 16 << 20),
        name="own_terms",
    )(first, second, tables)
    acc = pl.pallas_call(
        chunk_kernel,
        out_shape=acc_shape,
        in_specs=[VMEM] * 4,
        out_specs=VMEM,
        scratch_shapes=lists,
        input_output_aliases={3: 0},
        compiler_params=params(6),
        cost_estimate=cost(192 * term, 12 << 20),
        name="chunk_terms",
    )(in_vmem(b0), in_vmem(a0), tables, acc)
    out, _ = pl.pallas_call(
        last_kernel,
        out_shape=[jax.ShapeDtypeStruct((1, G, OWN, W), bf16), acc_shape],
        in_specs=[VMEM] * 4,
        out_specs=[HBM, VMEM],
        scratch_shapes=[pltpu.VMEM((G, OWN, W), bf16), dma] + lists,
        input_output_aliases={3: 1},
        compiler_params=params(6),
        cost_estimate=cost(64 * term, 4 << 20),
        name="last_terms",
    )(in_vmem(b1), in_vmem(a1), tables, acc)
    return jnp.transpose(out, (0, 2, 1, 3))


def solution(mesh):
    in_specs = (
        P("event", "dom", None, None, None),
        P("event", "dom", None, None),
        P("dom", "event", None),
        P(),
        P("dom", "event", None, None),
        P("dom", "event", None, None),
    )
    return jax.shard_map(
        per_device,
        mesh=mesh,
        in_specs=in_specs,
        out_specs=P("dom", "event", None, None),
        check_vma=False,
    )
```

```python
import jax
import jax.numpy as jnp
from jax import lax
from jax.experimental import pallas as pl
from jax.experimental.pallas import tpu as pltpu
from jax.sharding import PartitionSpec as P


OWN = 32
HALF = OWN // 2
G = 125
ADJ = G + 1
ROWS = 128
W = 128
PB = 16
U = 8
PAIR_ROWS = 3
OWN_LANE = 2 * OWN
MIB = 1 << 20
COPY_ALIASED = False


HBM = pl.BlockSpec(memory_space=pltpu.HBM)
VMEM = pl.BlockSpec(memory_space=pltpu.VMEM)
SMEM = pl.BlockSpec(memory_space=pltpu.SMEM)


def on_chip(shape, dtype):
    return pltpu.VMEM(shape, dtype)


def in_vmem(x):
    return pltpu.with_memory_space_constraint(x, pltpu.VMEM)


def in_hbm(x):
    return pltpu.with_memory_space_constraint(x, pltpu.HBM)


def params(mib):
    return pltpu.CompilerParams(vmem_limit_bytes=mib * MIB)


def cost(flops, nbytes):
    return pl.CostEstimate(flops=flops, bytes_accessed=nbytes, transcendentals=0)


PIECES = ((0, 32), (32, 32), (64, 32), (96, 29))


def partial_sums(kern, counts, base, out, buf, cbuf, sems, csem):
    copies = []
    for n, (first, size) in enumerate(PIECES):
        span = pl.ds(first, size)
        copies.append(
            pltpu.make_async_copy(
                kern.at[:, 0, span, pl.ds(base, OWN)], buf.at[:, span], sems.at[n]
            )
        )
    ccopy = pltpu.make_async_copy(counts.at[:, 0, pl.ds(base, OWN)], cbuf, csem)
    for copy in copies + [ccopy]:
        copy.start()
    yield
    for copy, (first, size) in zip(copies, PIECES):
        copy.wait()
        span = slice(first, first + size)
        total = buf[0, span].astype(jnp.float32) + buf[1, span].astype(jnp.float32)
        out[span] = total.astype(jnp.bfloat16)
    ccopy.wait()
    out[G] = (cbuf[0] + cbuf[1]).astype(jnp.float32).astype(jnp.bfloat16)


def send_kernel(kern, counts, out, *scratch):
    base = (1 - lax.axis_index("event")) * OWN
    for _ in partial_sums(kern, counts, base, out, *scratch):
        pass


def keep_kernel(kern, counts, off, tab, out, adj, *scratch):
    steps = partial_sums(kern, counts, lax.axis_index("event") * OWN, out, *scratch)
    next(steps)
    odd = lax.rem(lax.axis_index("dom"), 2)
    b = lax.broadcasted_iota(jnp.int32, (PB, OWN), 1)
    x = off[0, 0] + b
    part = x >> 5
    group = jnp.where(part == 1, 2, jnp.where(part == 0, odd, 1 - odd))
    lane = (x & (OWN - 1)) + group * OWN
    value = (tab[0, 0] + 1).astype(jnp.float32)
    spot = lax.broadcasted_iota(jnp.int32, (3 * OWN, OWN), 0)
    turned = jnp.zeros((3 * OWN, OWN), jnp.float32)
    for k in range(PB):
        turned = turned + jnp.where(spot == lane[k : k + 1], value[k : k + 1], 0.0)
    wide = jnp.concatenate([turned, jnp.zeros((OWN, OWN), jnp.float32)], axis=0)
    wide = jnp.concatenate([wide, jnp.zeros((W, W - OWN), jnp.float32)], axis=1)
    adj[...] = jnp.transpose(wide, (1, 0))[0:OWN]
    for _ in steps:
        pass


def source_kernel(own, got, vol, adj, first, second):
    odd = lax.rem(lax.axis_index("dom"), 2)
    for dst, half in ((first, odd), (second, 1 - odd)):
        span = pl.ds(pl.multiple_of(half * HALF, HALF), HALF)
        v = vol[0, span].astype(jnp.float32)
        hits = own[G, span].astype(jnp.float32) + got[G, span].astype(jnp.float32)
        factor = v / jnp.sqrt(1.0 + hits)
        total = own[0:G, span].astype(jnp.float32) + got[0:G, span].astype(jnp.float32)
        rest = pl.ds(pl.multiple_of((1 - half) * HALF, HALF), HALF)
        rows = [total * factor[None], v[None], adj[span][None], adj[rest][None]]
        block = jnp.concatenate(rows, axis=0)
        dst[...] = jnp.transpose(block, (1, 0, 2)).astype(jnp.bfloat16)


def neighbours(ref, row, lane):
    a = ref[:, row].astype(jnp.float32)
    return pltpu.roll(a, W - lane, 1) if lane else a


def make_lists(adj, lists):
    n = adj.shape[0]
    f32, bf16 = jnp.float32, jnp.bfloat16
    there = adj > 0.5
    ones = jnp.where(there, 1.0, 0.0)

    def triangle(m, strict):
        row = lax.broadcasted_iota(jnp.int32, (m, m), 0)
        col = lax.broadcasted_iota(jnp.int32, (m, m), 1)
        return jnp.where(col < row if strict else col <= row, 1.0, 0.0).astype(bf16)

    rank = jnp.dot(triangle(n, True), ones.astype(bf16), preferred_element_type=f32)
    rank = jnp.where(there, rank, -1.0)
    source = lax.broadcasted_iota(jnp.int32, (n, W), 0).astype(f32)
    code = source + 1.0 + 64.0 * (adj - 1.0)
    for r in range(n):
        picked = jnp.sum(jnp.where(rank == float(r), code, 0.0), axis=0, keepdims=True)
        lists[r : r + 1] = picked.astype(jnp.int32)
    terms = lax.dot_general(
        ones.astype(bf16), jnp.ones((n, W), bf16), (((0,), (0,)), ((), ())),
        preferred_element_type=f32,
    )[0:OWN]
    pairs = ((terms.astype(jnp.int32) + 1) >> 1).astype(f32)
    end = jnp.dot(triangle(OWN, False), pairs.astype(bf16), preferred_element_type=f32)
    lane = lax.broadcasted_iota(jnp.int32, (OWN, W), 1).astype(f32)
    for q in range(PAIR_ROWS):
        place = lane + float(q * W)
        past = end <= place
        target = jnp.sum(jnp.where(past, 1.0, 0.0), axis=0, keepdims=True)
        base = jnp.sum(jnp.where(past, pairs, 0.0), axis=0, keepdims=True)
        first = jnp.minimum(2.0 * (place[0:1] - base), float(n - 2))
        lists[n + q : n + q + 1] = (target + 256.0 * first).astype(jnp.int32)
    lists[n + PAIR_ROWS : n + PAIR_ROWS + 1] = end[OWN - 1 : OWN].astype(jnp.int32)


def list_rows(n):
    return n + 8


def add_terms(blocks, lists, tables, acc, mats, codes, sem):
    n = HALF * len(blocks)
    copy = pltpu.make_async_copy(lists, codes, sem)
    copy.start()
    mats[0] = jnp.zeros((ROWS, W), jnp.bfloat16)
    for i, ref in enumerate(blocks):
        mats[1 + i * HALF : 1 + (i + 1) * HALF] = ref[...]
    copy.wait()

    def step(i, carry):
        for u in range(U):
            at = i * U + u
            entry = codes[n + (at >> 7), at & (W - 1)]
            x, r = entry & 255, entry >> 8
            two = [codes[r + j, x] for j in range(2)]
            term = jnp.dot(
                jnp.concatenate([mats[c & 63] for c in two], axis=1),
                jnp.concatenate([tables[c >> 6] for c in two], axis=0),
                preferred_element_type=jnp.float32,
            )
            acc[x] = acc[x] + term
        return carry

    lax.fori_loop(0, (codes[n + PAIR_ROWS, 0] + (U - 1)) >> 3, step, 0)


def own_kernel(first, second, tables, acc, lists, *scratch):
    adj = [neighbours(first, ADJ, OWN_LANE), neighbours(second, ADJ, OWN_LANE)]
    make_lists(jnp.concatenate(adj, axis=0), lists)

    def clear(i, carry):
        acc[i] = jnp.zeros((ROWS, W), jnp.float32)
        return carry

    lax.fori_loop(0, OWN + 1, clear, 0)
    add_terms((first, second), lists, tables, acc, *scratch)


def chunk_kernel(from_b, from_a, tables, acc_in, acc, lists_a, lists_b, lists, *scratch):
    if COPY_ALIASED:
        acc[...] = acc_in[...]
    adj = [neighbours(from_b, ADJ, 0), neighbours(from_a, ADJ, OWN)]
    make_lists(jnp.concatenate(adj, axis=0), lists)
    make_lists(neighbours(from_a, ADJ + 1, OWN), lists_a)
    make_lists(neighbours(from_b, ADJ + 1, 0), lists_b)
    add_terms((from_b, from_a), lists, tables, acc, *scratch)


def finish(half, acc, out, stage, sems):
    copies = []
    for c in range(HALF // 8):
        first = pl.multiple_of(half * HALF + c * 8, 8)
        span = pl.ds(first, 8)
        scale = 1.0 / acc[span, G : G + 1]
        result = jnp.transpose(acc[span] * scale, (1, 0, 2))
        stage[c] = result[0:G].astype(jnp.bfloat16)
        copies.append(pltpu.make_async_copy(stage.at[c], out.at[0, :, span], sems.at[c]))
        copies[-1].start()
    for copy in copies:
        copy.wait()


def last_a_kernel(from_a, lists, tables, acc_in, out, acc, stage, sems, *scratch):
    if COPY_ALIASED:
        acc[...] = acc_in[...]
    add_terms((from_a,), lists, tables, acc, *scratch)
    finish(1 - lax.rem(lax.axis_index("dom"), 2), acc, out, stage, sems)


def last_b_kernel(from_b, lists, tables, acc_in, out_in, out, acc, stage, sems, *scratch):
    if COPY_ALIASED:
        acc[...] = acc_in[...]
        pltpu.sync_copy(out_in, out)
    add_terms((from_b,), lists, tables, acc, *scratch)
    finish(lax.rem(lax.axis_index("dom"), 2), acc, out, stage, sems)


def per_device(kernels, counts, volume, tables, pair_offset, pair_table):
    bf16, f32, i32 = jnp.bfloat16, jnp.float32, jnp.int32
    dma = pltpu.SemaphoreType.DMA
    kernels = in_hbm(jnp.transpose(kernels, (0, 1, 3, 2, 4)))
    counts = in_hbm(counts)
    pair_offset = jnp.transpose(pair_offset, (0, 1, 3, 2))
    pair_table = jnp.transpose(pair_table, (0, 1, 3, 2))
    sums = on_chip((G + 1, OWN, W), bf16)
    scratch = [
        pltpu.VMEM((2, G, OWN, W), bf16),
        pltpu.VMEM((2, OWN, W), i32),
        dma((len(PIECES),)),
        dma,
    ]

    to_other = pl.pallas_call(
        send_kernel,
        out_shape=sums,
        in_specs=[HBM, HBM],
        out_specs=VMEM,
        scratch_shapes=scratch,
        compiler_params=params(6),
        cost_estimate=cost(1 << 20, 4 << 20),
        name="send",
    )(kernels, counts)
    got = lax.ppermute(to_other, "event", [(0, 1), (1, 0)])
    own, adj = pl.pallas_call(
        keep_kernel,
        out_shape=[sums, on_chip((OWN, W), f32)],
        in_specs=[HBM, HBM, VMEM, VMEM],
        out_specs=[VMEM, VMEM],
        scratch_shapes=scratch,
        compiler_params=params(6),
        cost_estimate=cost(1 << 20, 4 << 20),
        name="keep",
    )(kernels, counts, pair_offset, pair_table)
    first, second = pl.pallas_call(
        source_kernel,
        out_shape=[on_chip((HALF, ROWS, W), bf16)] * 2,
        in_specs=[VMEM] * 4,
        out_specs=[VMEM] * 2,
        compiler_params=params(6),
        cost_estimate=cost(1 << 20, 4 << 20),
        name="source",
    )(own, in_vmem(got), volume, adj)

    count = lax.axis_size("dom")

    def swapped(value, start):
        pairs = [(a, a + 1) for a in range(start, count - 1, 2)]
        pairs = pairs + [(b, a) for a, b in pairs]
        return lax.ppermute(value, "dom", pairs)

    a0 = swapped(second, 0)
    b0 = swapped(first, 1)
    a1 = swapped(first, 0)
    b1 = swapped(second, 1)

    acc_shape = on_chip((OWN + 1, ROWS, W), f32)
    out_shape = jax.ShapeDtypeStruct((1, G, OWN, W), bf16)
    term = 2 * ROWS * W * W

    def lists(n):
        return (list_rows(n), W)

    def work(n):
        return [pltpu.VMEM((n + 1, ROWS, W), bf16), pltpu.SMEM(lists(n), i32), dma]

    stage = [pltpu.VMEM((HALF // 8, G, 8, W), bf16), dma((HALF // 8,))]
    acc = pl.pallas_call(
        own_kernel,
        out_shape=acc_shape,
        in_specs=[VMEM] * 3,
        out_specs=VMEM,
        scratch_shapes=[pltpu.VMEM(lists(OWN), i32)] + work(OWN),
        compiler_params=params(6),
        cost_estimate=cost(256 * term, 16 << 20),
        name="own_terms",
    )(first, second, tables)
    acc, lists_a, lists_b = pl.pallas_call(
        chunk_kernel,
        out_shape=[acc_shape] + [on_chip(lists(HALF), i32)] * 2,
        in_specs=[VMEM] * 4,
        out_specs=[VMEM] * 3,
        scratch_shapes=[pltpu.VMEM(lists(OWN), i32)] + work(OWN),
        input_output_aliases={3: 0},
        compiler_params=params(6),
        cost_estimate=cost(192 * term, 12 << 20),
        name="chunk_terms",
    )(in_vmem(b0), in_vmem(a0), tables, acc)
    out, acc = pl.pallas_call(
        last_a_kernel,
        out_shape=[out_shape, acc_shape],
        in_specs=[VMEM] * 4,
        out_specs=[HBM, VMEM],
        scratch_shapes=stage + work(HALF),
        input_output_aliases={3: 1},
        compiler_params=params(6),
        cost_estimate=cost(32 * term, 2 << 20),
        name="last_a",
    )(in_vmem(a1), lists_a, tables, acc)
    out, _ = pl.pallas_call(
        last_b_kernel,
        out_shape=[out_shape, acc_shape],
        in_specs=[VMEM] * 4 + [HBM],
        out_specs=[HBM, VMEM],
        scratch_shapes=stage + work(HALF),
        input_output_aliases={3: 1, 4: 0},
        compiler_params=params(6),
        cost_estimate=cost(32 * term, 2 << 20),
        name="last_b",
    )(in_vmem(b1), lists_b, tables, acc, out)
    return jnp.transpose(out, (0, 2, 1, 3))


def solution(mesh):
    in_specs = (
        P("event", "dom", None, None, None),
        P("event", "dom", None, None),
        P("dom", "event", None),
        P(),
        P("dom", "event", None, None),
        P("dom", "event", None, None),
    )
    return jax.shard_map(
        per_device,
        mesh=mesh,
        in_specs=in_specs,
        out_specs=P("dom", "event", None, None),
        check_vma=False,
    )
```

```python
import functools

import jax
import jax.numpy as jnp
from jax import lax
from jax.experimental import pallas as pl
from jax.experimental.pallas import tpu as pltpu
from jax.sharding import PartitionSpec as P


OWN = 32
HALF = OWN // 2
G = 125
ADJ = G + 1
ROWS = 128
W = 128
PB = 16
U = 8
PAIR_ROWS = 3
PREV_LANE, OWN_LANE, NEXT_LANE = 0, OWN, 2 * OWN
MIB = 1 << 20
COPY_ALIASED = False


HBM = pl.BlockSpec(memory_space=pltpu.HBM)
VMEM = pl.BlockSpec(memory_space=pltpu.VMEM)
SMEM = pl.BlockSpec(memory_space=pltpu.SMEM)


def on_chip(shape, dtype):
    return pltpu.VMEM(shape, dtype)


def in_vmem(x):
    return pltpu.with_memory_space_constraint(x, pltpu.VMEM)


def in_hbm(x):
    return pltpu.with_memory_space_constraint(x, pltpu.HBM)


def params(mib):
    return pltpu.CompilerParams(vmem_limit_bytes=mib * MIB)


def shifted(value, axis, steps):
    count = lax.axis_size(axis)
    first, last = (max(0, -steps), min(count, count - steps))
    return lax.ppermute(value, axis, [(source, source + steps) for source in range(first, last)])


def cost(flops, nbytes):
    return pl.CostEstimate(flops=flops, bytes_accessed=nbytes, transcendentals=0)


PIECES = tuple((first, min(16, G - first)) for first in range(0, G, 16))


def partial_sums(kern, counts, base, out, buf, cbuf, sems, csem):
    copies = []
    for n, (first, size) in enumerate(PIECES):
        span = pl.ds(first, size)
        copies.append(
            pltpu.make_async_copy(
                kern.at[:, 0, span, pl.ds(base, OWN)], buf.at[:, span], sems.at[n]
            )
        )
    ccopy = pltpu.make_async_copy(counts.at[:, 0, pl.ds(base, OWN)], cbuf, csem)
    for copy in copies + [ccopy]:
        copy.start()
    yield
    for copy, (first, size) in zip(copies, PIECES):
        copy.wait()
        span = slice(first, first + size)
        total = buf[0, span].astype(jnp.float32) + buf[1, span].astype(jnp.float32)
        out[span] = total.astype(jnp.bfloat16)
    ccopy.wait()
    out[G] = (cbuf[0] + cbuf[1]).astype(jnp.float32).astype(jnp.bfloat16)


def send_kernel(kern, counts, out, *scratch):
    base = (1 - lax.axis_index("event")) * OWN
    for _ in partial_sums(kern, counts, base, out, *scratch):
        pass


def keep_kernel(kern, counts, off, tab, out, adj, *scratch):
    steps = partial_sums(kern, counts, lax.axis_index("event") * OWN, out, *scratch)
    next(steps)
    b = lax.broadcasted_iota(jnp.int32, (PB, OWN), 1)
    lane = off[0, 0] + b
    value = (tab[0, 0] + 1).astype(jnp.float32)
    spot = lax.broadcasted_iota(jnp.int32, (3 * OWN, OWN), 0)
    turned = jnp.zeros((3 * OWN, OWN), jnp.float32)
    for k in range(PB):
        turned = turned + jnp.where(spot == lane[k : k + 1], value[k : k + 1], 0.0)
    wide = jnp.concatenate([turned, jnp.zeros((OWN, OWN), jnp.float32)], axis=0)
    wide = jnp.concatenate([wide, jnp.zeros((W, W - OWN), jnp.float32)], axis=1)
    adj[...] = jnp.transpose(wide, (1, 0))[0:OWN]
    for _ in steps:
        pass


def source_kernel(half, own, got, vol, adj, dst):
    span = slice(half * HALF, (half + 1) * HALF)
    rest = slice((1 - half) * HALF, (2 - half) * HALF)
    v = vol[0, span].astype(jnp.float32)
    hits = own[G, span].astype(jnp.float32) + got[G, span].astype(jnp.float32)
    factor = v / jnp.sqrt(1.0 + hits)
    total = own[0:G, span].astype(jnp.float32) + got[0:G, span].astype(jnp.float32)
    rows = [total * factor[None], v[None], adj[span][None], adj[rest][None]]
    block = jnp.concatenate(rows, axis=0)
    dst[...] = jnp.transpose(block, (1, 0, 2)).astype(jnp.bfloat16)


def neighbours(ref, row, lane):
    a = ref[:, row].astype(jnp.float32)
    return pltpu.roll(a, W - lane, 1) if lane else a


def make_lists(adj, lists):
    n = adj.shape[0]
    f32, bf16 = jnp.float32, jnp.bfloat16
    there = adj > 0.5
    ones = jnp.where(there, 1.0, 0.0)

    def triangle(m, strict):
        row = lax.broadcasted_iota(jnp.int32, (m, m), 0)
        col = lax.broadcasted_iota(jnp.int32, (m, m), 1)
        return jnp.where(col < row if strict else col <= row, 1.0, 0.0).astype(bf16)

    rank = jnp.dot(triangle(n, True), ones.astype(bf16), preferred_element_type=f32)
    rank = jnp.where(there, rank, -1.0)
    source = lax.broadcasted_iota(jnp.int32, (n, W), 0).astype(f32)
    code = source + 1.0 + 64.0 * (adj - 1.0)
    for r in range(n):
        picked = jnp.sum(jnp.where(rank == float(r), code, 0.0), axis=0, keepdims=True)
        lists[r : r + 1] = picked.astype(jnp.int32)
    terms = lax.dot_general(
        ones.astype(bf16), jnp.ones((n, W), bf16), (((0,), (0,)), ((), ())),
        preferred_element_type=f32,
    )[0:OWN]
    pairs = ((terms.astype(jnp.int32) + 1) >> 1).astype(f32)
    end = jnp.dot(triangle(OWN, False), pairs.astype(bf16), preferred_element_type=f32)
    lane = lax.broadcasted_iota(jnp.int32, (OWN, W), 1).astype(f32)
    for q in range(PAIR_ROWS):
        place = lane + float(q * W)
        past = end <= place
        target = jnp.sum(jnp.where(past, 1.0, 0.0), axis=0, keepdims=True)
        base = jnp.sum(jnp.where(past, pairs, 0.0), axis=0, keepdims=True)
        first = jnp.minimum(2.0 * (place[0:1] - base), float(n - 2))
        lists[n + q : n + q + 1] = (target + 256.0 * first).astype(jnp.int32)
    lists[n + PAIR_ROWS : n + PAIR_ROWS + 1] = end[OWN - 1 : OWN].astype(jnp.int32)


def list_rows(n):
    return n + 8


def add_terms(blocks, lists, tables, acc, mats, codes, sem):
    n = HALF * len(blocks)
    copy = pltpu.make_async_copy(lists, codes, sem)
    copy.start()
    mats[0] = jnp.zeros((ROWS, W), jnp.bfloat16)
    for i, ref in enumerate(blocks):
        mats[1 + i * HALF : 1 + (i + 1) * HALF] = ref[...]
    copy.wait()

    def step(i, carry):
        for u in range(U):
            at = i * U + u
            entry = codes[n + (at >> 7), at & (W - 1)]
            x, r = entry & 255, entry >> 8
            two = [codes[r + j, x] for j in range(2)]
            term = jnp.dot(
                jnp.concatenate([mats[c & 63] for c in two], axis=1),
                jnp.concatenate([tables[c >> 6] for c in two], axis=0),
                preferred_element_type=jnp.float32,
            )
            acc[x] = acc[x] + term
        return carry

    lax.fori_loop(0, (codes[n + PAIR_ROWS, 0] + (U - 1)) >> 3, step, 0)


def own_kernel(low, high, tables, acc, lists, *scratch):
    adj = [neighbours(low, ADJ, OWN_LANE), neighbours(high, ADJ, OWN_LANE)]
    make_lists(jnp.concatenate(adj, axis=0), lists)

    def clear(i, carry):
        acc[i] = jnp.zeros((ROWS, W), jnp.float32)
        return carry

    lax.fori_loop(0, OWN + 1, clear, 0)
    add_terms((low, high), lists, tables, acc, *scratch)


def chunk_kernel(from_next, from_prev, tables, acc_in, acc, lists_n, lists_p, lists, *scratch):
    if COPY_ALIASED:
        acc[...] = acc_in[...]
    adj = [neighbours(from_next, ADJ, PREV_LANE), neighbours(from_prev, ADJ, NEXT_LANE)]
    make_lists(jnp.concatenate(adj, axis=0), lists)
    make_lists(neighbours(from_next, ADJ + 1, PREV_LANE), lists_n)
    make_lists(neighbours(from_prev, ADJ + 1, NEXT_LANE), lists_p)
    add_terms((from_next, from_prev), lists, tables, acc, *scratch)


def finish(half, acc, out, stage, sems):
    copies = []
    for c in range(HALF // 8):
        span = slice(half * HALF + c * 8, half * HALF + c * 8 + 8)
        scale = 1.0 / acc[span, G : G + 1]
        result = jnp.transpose(acc[span] * scale, (1, 0, 2))
        stage[c] = result[0:G].astype(jnp.bfloat16)
        copies.append(pltpu.make_async_copy(stage.at[c], out.at[0, :, span], sems.at[c]))
        copies[-1].start()
    for copy in copies:
        copy.wait()


def last_n_kernel(source, lists, tables, acc_in, out, acc, stage, sems, *scratch):
    if COPY_ALIASED:
        acc[...] = acc_in[...]
    add_terms((source,), lists, tables, acc, *scratch)
    finish(1, acc, out, stage, sems)


def last_p_kernel(source, lists, tables, acc_in, out_in, out, acc, stage, sems, *scratch):
    if COPY_ALIASED:
        acc[...] = acc_in[...]
        pltpu.sync_copy(out_in, out)
    add_terms((source,), lists, tables, acc, *scratch)
    finish(0, acc, out, stage, sems)


def per_device(kernels, counts, volume, tables, pair_offset, pair_table):
    bf16, f32, i32 = jnp.bfloat16, jnp.float32, jnp.int32
    dma = pltpu.SemaphoreType.DMA
    kernels = in_hbm(jnp.transpose(kernels, (0, 1, 3, 2, 4)))
    counts = in_hbm(counts)
    pair_offset = jnp.transpose(pair_offset, (0, 1, 3, 2))
    pair_table = jnp.transpose(pair_table, (0, 1, 3, 2))
    sums = on_chip((G + 1, OWN, W), bf16)
    scratch = [
        pltpu.VMEM((2, G, OWN, W), bf16),
        pltpu.VMEM((2, OWN, W), i32),
        dma((len(PIECES),)),
        dma,
    ]

    to_other = pl.pallas_call(
        send_kernel,
        out_shape=sums,
        in_specs=[HBM, HBM],
        out_specs=VMEM,
        scratch_shapes=scratch,
        compiler_params=params(6),
        cost_estimate=cost(1 << 20, 4 << 20),
        name="send",
    )(kernels, counts)
    got = lax.ppermute(to_other, "event", [(0, 1), (1, 0)])
    own, adj = pl.pallas_call(
        keep_kernel,
        out_shape=[sums, on_chip((OWN, W), f32)],
        in_specs=[HBM, HBM, VMEM, VMEM],
        out_specs=[VMEM, VMEM],
        scratch_shapes=scratch,
        compiler_params=params(6),
        cost_estimate=cost(1 << 20, 4 << 20),
        name="keep",
    )(kernels, counts, pair_offset, pair_table)

    def source(half):
        return pl.pallas_call(
            functools.partial(source_kernel, half),
            out_shape=on_chip((HALF, ROWS, W), bf16),
            in_specs=[VMEM] * 4,
            out_specs=VMEM,
            compiler_params=params(6),
            cost_estimate=cost(1 << 20, 2 << 20),
        )(own, in_vmem(got), volume, adj)

    def moved(value, steps):
        return in_vmem(shifted(value, "dom", steps))

    high = source(1)
    p0 = moved(high, 1)
    low = source(0)
    n0 = moved(low, -1)
    p1 = moved(low, 1)
    n1 = moved(high, -1)

    acc_shape = on_chip((OWN + 1, ROWS, W), f32)
    out_shape = jax.ShapeDtypeStruct((1, G, OWN, W), bf16)
    term = 2 * ROWS * W * W

    def lists(n):
        return (list_rows(n), W)

    def work(n):
        return [pltpu.VMEM((n + 1, ROWS, W), bf16), pltpu.SMEM(lists(n), i32), dma]

    stage = [pltpu.VMEM((HALF // 8, G, 8, W), bf16), dma((HALF // 8,))]
    acc = pl.pallas_call(
        own_kernel,
        out_shape=acc_shape,
        in_specs=[VMEM] * 3,
        out_specs=VMEM,
        scratch_shapes=[pltpu.VMEM(lists(OWN), i32)] + work(OWN),
        compiler_params=params(6),
        cost_estimate=cost(256 * term, 16 << 20),
        name="own_terms",
    )(low, high, tables)
    acc, lists_n, lists_p = pl.pallas_call(
        chunk_kernel,
        out_shape=[acc_shape] + [on_chip(lists(HALF), i32)] * 2,
        in_specs=[VMEM] * 4,
        out_specs=[VMEM] * 3,
        scratch_shapes=[pltpu.VMEM(lists(OWN), i32)] + work(OWN),
        input_output_aliases={3: 0},
        compiler_params=params(6),
        cost_estimate=cost(192 * term, 12 << 20),
        name="chunk_terms",
    )(n0, p0, tables, acc)
    out, acc = pl.pallas_call(
        last_n_kernel,
        out_shape=[out_shape, acc_shape],
        in_specs=[VMEM] * 4,
        out_specs=[HBM, VMEM],
        scratch_shapes=stage + work(HALF),
        input_output_aliases={3: 1},
        compiler_params=params(6),
        cost_estimate=cost(32 * term, 2 << 20),
        name="last_n",
    )(n1, lists_n, tables, acc)
    out, _ = pl.pallas_call(
        last_p_kernel,
        out_shape=[out_shape, acc_shape],
        in_specs=[VMEM] * 4 + [HBM],
        out_specs=[HBM, VMEM],
        scratch_shapes=stage + work(HALF),
        input_output_aliases={3: 1, 4: 0},
        compiler_params=params(6),
        cost_estimate=cost(32 * term, 2 << 20),
        name="last_p",
    )(p1, lists_p, tables, acc, out)
    return jnp.transpose(out, (0, 2, 1, 3))


def solution(mesh):
    in_specs = (
        P("event", "dom", None, None, None),
        P("event", "dom", None, None),
        P("dom", "event", None),
        P(),
        P("dom", "event", None, None),
        P("dom", "event", None, None),
    )
    return jax.shard_map(
        per_device,
        mesh=mesh,
        in_specs=in_specs,
        out_specs=P("dom", "event", None, None),
        check_vma=False,
    )
```

```python
import functools

import jax
import jax.numpy as jnp
from jax import lax
from jax.experimental import pallas as pl
from jax.experimental.pallas import tpu as pltpu
from jax.sharding import PartitionSpec as P


OWN = 32
HALF = OWN // 2
G = 125
ADJ = G + 1
ROWS = 128
W = 128
PB = 16
U = 8
PAIR_ROWS = 3
OWN_LANE = 2 * OWN
MIB = 1 << 20
COPY_ALIASED = False


HBM = pl.BlockSpec(memory_space=pltpu.HBM)
VMEM = pl.BlockSpec(memory_space=pltpu.VMEM)
SMEM = pl.BlockSpec(memory_space=pltpu.SMEM)


def on_chip(shape, dtype):
    return pltpu.VMEM(shape, dtype)


def in_vmem(x):
    return pltpu.with_memory_space_constraint(x, pltpu.VMEM)


def in_hbm(x):
    return pltpu.with_memory_space_constraint(x, pltpu.HBM)


def params(mib):
    return pltpu.CompilerParams(vmem_limit_bytes=mib * MIB)


def cost(flops, nbytes):
    return pl.CostEstimate(flops=flops, bytes_accessed=nbytes, transcendentals=0)


PIECES = tuple((first, min(16, G - first)) for first in range(0, G, 16))


def partial_sums(kern, counts, base, out, buf, cbuf, sems, csem):
    copies = []
    for n, (first, size) in enumerate(PIECES):
        span = pl.ds(first, size)
        copies.append(
            pltpu.make_async_copy(
                kern.at[:, 0, span, pl.ds(base, OWN)], buf.at[:, span], sems.at[n]
            )
        )
    ccopy = pltpu.make_async_copy(counts.at[:, 0, pl.ds(base, OWN)], cbuf, csem)
    for copy in copies + [ccopy]:
        copy.start()
    yield
    for copy, (first, size) in zip(copies, PIECES):
        copy.wait()
        span = slice(first, first + size)
        total = buf[0, span].astype(jnp.float32) + buf[1, span].astype(jnp.float32)
        out[span] = total.astype(jnp.bfloat16)
    ccopy.wait()
    out[G] = (cbuf[0] + cbuf[1]).astype(jnp.float32).astype(jnp.bfloat16)


def send_kernel(kern, counts, out, *scratch):
    base = (1 - lax.axis_index("event")) * OWN
    for _ in partial_sums(kern, counts, base, out, *scratch):
        pass


def keep_kernel(kern, counts, off, tab, out, adj, *scratch):
    steps = partial_sums(kern, counts, lax.axis_index("event") * OWN, out, *scratch)
    next(steps)
    odd = lax.rem(lax.axis_index("dom"), 2)
    b = lax.broadcasted_iota(jnp.int32, (PB, OWN), 1)
    x = off[0, 0] + b
    part = x >> 5
    group = jnp.where(part == 1, 2, jnp.where(part == 0, odd, 1 - odd))
    lane = (x & (OWN - 1)) + group * OWN
    value = (tab[0, 0] + 1).astype(jnp.float32)
    spot = lax.broadcasted_iota(jnp.int32, (3 * OWN, OWN), 0)
    turned = jnp.zeros((3 * OWN, OWN), jnp.float32)
    for k in range(PB):
        turned = turned + jnp.where(spot == lane[k : k + 1], value[k : k + 1], 0.0)
    wide = jnp.concatenate([turned, jnp.zeros((OWN, OWN), jnp.float32)], axis=0)
    wide = jnp.concatenate([wide, jnp.zeros((W, W - OWN), jnp.float32)], axis=1)
    adj[...] = jnp.transpose(wide, (1, 0))[0:OWN]
    for _ in steps:
        pass


def source_kernel(leaves_first, own, got, vol, adj, dst):
    odd = lax.rem(lax.axis_index("dom"), 2)
    half = odd if leaves_first else 1 - odd
    span = pl.ds(pl.multiple_of(half * HALF, HALF), HALF)
    rest = pl.ds(pl.multiple_of((1 - half) * HALF, HALF), HALF)
    v = vol[0, span].astype(jnp.float32)
    hits = own[G, span].astype(jnp.float32) + got[G, span].astype(jnp.float32)
    factor = v / jnp.sqrt(1.0 + hits)
    total = own[0:G, span].astype(jnp.float32) + got[0:G, span].astype(jnp.float32)
    rows = [total * factor[None], v[None], adj[span][None], adj[rest][None]]
    block = jnp.concatenate(rows, axis=0)
    dst[...] = jnp.transpose(block, (1, 0, 2)).astype(jnp.bfloat16)


def neighbours(ref, row, lane):
    a = ref[:, row].astype(jnp.float32)
    return pltpu.roll(a, W - lane, 1) if lane else a


def make_lists(adj, lists):
    n = adj.shape[0]
    f32, bf16 = jnp.float32, jnp.bfloat16
    there = adj > 0.5
    ones = jnp.where(there, 1.0, 0.0)

    def triangle(m, strict):
        row = lax.broadcasted_iota(jnp.int32, (m, m), 0)
        col = lax.broadcasted_iota(jnp.int32, (m, m), 1)
        return jnp.where(col < row if strict else col <= row, 1.0, 0.0).astype(bf16)

    rank = jnp.dot(triangle(n, True), ones.astype(bf16), preferred_element_type=f32)
    rank = jnp.where(there, rank, -1.0)
    source = lax.broadcasted_iota(jnp.int32, (n, W), 0).astype(f32)
    code = source + 1.0 + 64.0 * (adj - 1.0)
    for r in range(n):
        picked = jnp.sum(jnp.where(rank == float(r), code, 0.0), axis=0, keepdims=True)
        lists[r : r + 1] = picked.astype(jnp.int32)
    terms = lax.dot_general(
        ones.astype(bf16), jnp.ones((n, W), bf16), (((0,), (0,)), ((), ())),
        preferred_element_type=f32,
    )[0:OWN]
    pairs = ((terms.astype(jnp.int32) + 1) >> 1).astype(f32)
    end = jnp.dot(triangle(OWN, False), pairs.astype(bf16), preferred_element_type=f32)
    lane = lax.broadcasted_iota(jnp.int32, (OWN, W), 1).astype(f32)
    for q in range(PAIR_ROWS):
        place = lane + float(q * W)
        past = end <= place
        target = jnp.sum(jnp.where(past, 1.0, 0.0), axis=0, keepdims=True)
        base = jnp.sum(jnp.where(past, pairs, 0.0), axis=0, keepdims=True)
        first = jnp.minimum(2.0 * (place[0:1] - base), float(n - 2))
        lists[n + q : n + q + 1] = (target + 256.0 * first).astype(jnp.int32)
    lists[n + PAIR_ROWS : n + PAIR_ROWS + 1] = end[OWN - 1 : OWN].astype(jnp.int32)


def list_rows(n):
    return n + 8


def add_terms(blocks, lists, tables, acc, mats, codes, sem):
    n = HALF * len(blocks)
    copy = pltpu.make_async_copy(lists, codes, sem)
    copy.start()
    mats[0] = jnp.zeros((ROWS, W), jnp.bfloat16)
    for i, ref in enumerate(blocks):
        mats[1 + i * HALF : 1 + (i + 1) * HALF] = ref[...]
    copy.wait()

    def step(i, carry):
        for u in range(U):
            at = i * U + u
            entry = codes[n + (at >> 7), at & (W - 1)]
            x, r = entry & 255, entry >> 8
            two = [codes[r + j, x] for j in range(2)]
            term = jnp.dot(
                jnp.concatenate([mats[c & 63] for c in two], axis=1),
                jnp.concatenate([tables[c >> 6] for c in two], axis=0),
                preferred_element_type=jnp.float32,
            )
            acc[x] = acc[x] + term
        return carry

    lax.fori_loop(0, (codes[n + PAIR_ROWS, 0] + (U - 1)) >> 3, step, 0)


def own_kernel(first, second, tables, acc, lists, *scratch):
    adj = [neighbours(first, ADJ, OWN_LANE), neighbours(second, ADJ, OWN_LANE)]
    make_lists(jnp.concatenate(adj, axis=0), lists)

    def clear(i, carry):
        acc[i] = jnp.zeros((ROWS, W), jnp.float32)
        return carry

    lax.fori_loop(0, OWN + 1, clear, 0)
    add_terms((first, second), lists, tables, acc, *scratch)


def chunk_kernel(from_b, from_a, tables, acc_in, acc, lists_a, lists_b, lists, *scratch):
    if COPY_ALIASED:
        acc[...] = acc_in[...]
    adj = [neighbours(from_b, ADJ, 0), neighbours(from_a, ADJ, OWN)]
    make_lists(jnp.concatenate(adj, axis=0), lists)
    make_lists(neighbours(from_a, ADJ + 1, OWN), lists_a)
    make_lists(neighbours(from_b, ADJ + 1, 0), lists_b)
    add_terms((from_b, from_a), lists, tables, acc, *scratch)


def finish(half, acc, out, stage, sems):
    copies = []
    for c in range(HALF // 8):
        first = pl.multiple_of(half * HALF + c * 8, 8)
        span = pl.ds(first, 8)
        scale = 1.0 / acc[span, G : G + 1]
        result = jnp.transpose(acc[span] * scale, (1, 0, 2))
        stage[c] = result[0:G].astype(jnp.bfloat16)
        copies.append(pltpu.make_async_copy(stage.at[c], out.at[0, :, span], sems.at[c]))
        copies[-1].start()
    for copy in copies:
        copy.wait()


def last_b_kernel(from_b, lists, tables, acc_in, out, acc, stage, sems, *scratch):
    if COPY_ALIASED:
        acc[...] = acc_in[...]
    add_terms((from_b,), lists, tables, acc, *scratch)
    finish(lax.rem(lax.axis_index("dom"), 2), acc, out, stage, sems)


def last_a_kernel(from_a, lists, tables, acc_in, out_in, out, acc, stage, sems, *scratch):
    if COPY_ALIASED:
        acc[...] = acc_in[...]
        pltpu.sync_copy(out_in, out)
    add_terms((from_a,), lists, tables, acc, *scratch)
    finish(1 - lax.rem(lax.axis_index("dom"), 2), acc, out, stage, sems)


def per_device(kernels, counts, volume, tables, pair_offset, pair_table):
    bf16, f32, i32 = jnp.bfloat16, jnp.float32, jnp.int32
    dma = pltpu.SemaphoreType.DMA
    kernels = in_hbm(jnp.transpose(kernels, (0, 1, 3, 2, 4)))
    counts = in_hbm(counts)
    pair_offset = jnp.transpose(pair_offset, (0, 1, 3, 2))
    pair_table = jnp.transpose(pair_table, (0, 1, 3, 2))
    sums = on_chip((G + 1, OWN, W), bf16)
    scratch = [
        pltpu.VMEM((2, G, OWN, W), bf16),
        pltpu.VMEM((2, OWN, W), i32),
        dma((len(PIECES),)),
        dma,
    ]

    to_other = pl.pallas_call(
        send_kernel,
        out_shape=sums,
        in_specs=[HBM, HBM],
        out_specs=VMEM,
        scratch_shapes=scratch,
        compiler_params=params(6),
        cost_estimate=cost(1 << 20, 4 << 20),
        name="send",
    )(kernels, counts)
    got = lax.ppermute(to_other, "event", [(0, 1), (1, 0)])
    own, adj = pl.pallas_call(
        keep_kernel,
        out_shape=[sums, on_chip((OWN, W), f32)],
        in_specs=[HBM, HBM, VMEM, VMEM],
        out_specs=[VMEM, VMEM],
        scratch_shapes=scratch,
        compiler_params=params(6),
        cost_estimate=cost(1 << 20, 4 << 20),
        name="keep",
    )(kernels, counts, pair_offset, pair_table)

    def source(leaves_first):
        return pl.pallas_call(
            functools.partial(source_kernel, leaves_first),
            out_shape=on_chip((HALF, ROWS, W), bf16),
            in_specs=[VMEM] * 4,
            out_specs=VMEM,
            compiler_params=params(6),
            cost_estimate=cost(1 << 20, 2 << 20),
        )(own, in_vmem(got), volume, adj)

    count = lax.axis_size("dom")

    def swapped(value, start):
        pairs = [(a, a + 1) for a in range(start, count - 1, 2)]
        pairs = pairs + [(b, a) for a, b in pairs]
        return in_vmem(lax.ppermute(value, "dom", pairs))

    first = source(True)
    b0 = swapped(first, 1)
    second = source(False)
    a0 = swapped(second, 0)
    b1 = swapped(second, 1)
    a1 = swapped(first, 0)

    acc_shape = on_chip((OWN + 1, ROWS, W), f32)
    out_shape = jax.ShapeDtypeStruct((1, G, OWN, W), bf16)
    term = 2 * ROWS * W * W

    def lists(n):
        return (list_rows(n), W)

    def work(n):
        return [pltpu.VMEM((n + 1, ROWS, W), bf16), pltpu.SMEM(lists(n), i32), dma]

    stage = [pltpu.VMEM((HALF // 8, G, 8, W), bf16), dma((HALF // 8,))]
    acc = pl.pallas_call(
        own_kernel,
        out_shape=acc_shape,
        in_specs=[VMEM] * 3,
        out_specs=VMEM,
        scratch_shapes=[pltpu.VMEM(lists(OWN), i32)] + work(OWN),
        compiler_params=params(6),
        cost_estimate=cost(256 * term, 16 << 20),
        name="own_terms",
    )(first, second, tables)
    acc, lists_a, lists_b = pl.pallas_call(
        chunk_kernel,
        out_shape=[acc_shape] + [on_chip(lists(HALF), i32)] * 2,
        in_specs=[VMEM] * 4,
        out_specs=[VMEM] * 3,
        scratch_shapes=[pltpu.VMEM(lists(OWN), i32)] + work(OWN),
        input_output_aliases={3: 0},
        compiler_params=params(6),
        cost_estimate=cost(192 * term, 12 << 20),
        name="chunk_terms",
    )(b0, a0, tables, acc)
    out, acc = pl.pallas_call(
        last_b_kernel,
        out_shape=[out_shape, acc_shape],
        in_specs=[VMEM] * 4,
        out_specs=[HBM, VMEM],
        scratch_shapes=stage + work(HALF),
        input_output_aliases={3: 1},
        compiler_params=params(6),
        cost_estimate=cost(32 * term, 2 << 20),
        name="last_b",
    )(b1, lists_b, tables, acc)
    out, _ = pl.pallas_call(
        last_a_kernel,
        out_shape=[out_shape, acc_shape],
        in_specs=[VMEM] * 4 + [HBM],
        out_specs=[HBM, VMEM],
        scratch_shapes=stage + work(HALF),
        input_output_aliases={3: 1, 4: 0},
        compiler_params=params(6),
        cost_estimate=cost(32 * term, 2 << 20),
        name="last_a",
    )(a1, lists_a, tables, acc, out)
    return jnp.transpose(out, (0, 2, 1, 3))


def solution(mesh):
    in_specs = (
        P("event", "dom", None, None, None),
        P("event", "dom", None, None),
        P("dom", "event", None),
        P(),
        P("dom", "event", None, None),
        P("dom", "event", None, None),
    )
    return jax.shard_map(
        per_device,
        mesh=mesh,
        in_specs=in_specs,
        out_specs=P("dom", "event", None, None),
        check_vma=False,
    )
```

```python
import jax
import jax.numpy as jnp
from jax import lax
from jax.experimental import pallas as pl
from jax.experimental.pallas import tpu as pltpu
from jax.sharding import PartitionSpec as P


OWN = 32
HALF = OWN // 2
REST = 8
BIG = OWN - REST
G = 125
ADJ = G + 1
ROWS = 128
W = 128
PB = 16
U = 8
PAIR_ROWS = 3
OWN_LANE = 2 * OWN
MIB = 1 << 20
COPY_ALIASED = False


HBM = pl.BlockSpec(memory_space=pltpu.HBM)
VMEM = pl.BlockSpec(memory_space=pltpu.VMEM)
SMEM = pl.BlockSpec(memory_space=pltpu.SMEM)


def on_chip(shape, dtype):
    return pltpu.VMEM(shape, dtype)


def in_vmem(x):
    return pltpu.with_memory_space_constraint(x, pltpu.VMEM)


def in_hbm(x):
    return pltpu.with_memory_space_constraint(x, pltpu.HBM)


def params(mib):
    return pltpu.CompilerParams(vmem_limit_bytes=mib * MIB)


def cost(flops, nbytes):
    return pl.CostEstimate(flops=flops, bytes_accessed=nbytes, transcendentals=0)


PIECES = tuple((first, min(16, G - first)) for first in range(0, G, 16))


def partial_sums(kern, counts, base, out, buf, cbuf, sems, csem):
    copies = []
    for n, (first, size) in enumerate(PIECES):
        span = pl.ds(first, size)
        copies.append(
            pltpu.make_async_copy(
                kern.at[:, 0, span, pl.ds(base, OWN)], buf.at[:, span], sems.at[n]
            )
        )
    ccopy = pltpu.make_async_copy(counts.at[:, 0, pl.ds(base, OWN)], cbuf, csem)
    for copy in copies + [ccopy]:
        copy.start()
    yield
    for copy, (first, size) in zip(copies, PIECES):
        copy.wait()
        span = slice(first, first + size)
        total = buf[0, span].astype(jnp.float32) + buf[1, span].astype(jnp.float32)
        out[span] = total.astype(jnp.bfloat16)
    ccopy.wait()
    out[G] = (cbuf[0] + cbuf[1]).astype(jnp.float32).astype(jnp.bfloat16)


def send_kernel(kern, counts, out, *scratch):
    base = (1 - lax.axis_index("event")) * OWN
    for _ in partial_sums(kern, counts, base, out, *scratch):
        pass


def keep_kernel(kern, counts, off, tab, out, adj, *scratch):
    steps = partial_sums(kern, counts, lax.axis_index("event") * OWN, out, *scratch)
    next(steps)
    odd = lax.rem(lax.axis_index("dom"), 2)
    b = lax.broadcasted_iota(jnp.int32, (PB, OWN), 1)
    x = off[0, 0] + b
    part = x >> 5
    group = jnp.where(part == 1, 2, jnp.where(part == 0, odd, 1 - odd))
    lane = (x & (OWN - 1)) + group * OWN
    value = (tab[0, 0] + 1).astype(jnp.float32)
    spot = lax.broadcasted_iota(jnp.int32, (3 * OWN, OWN), 0)
    turned = jnp.zeros((3 * OWN, OWN), jnp.float32)
    for k in range(PB):
        turned = turned + jnp.where(spot == lane[k : k + 1], value[k : k + 1], 0.0)
    wide = jnp.concatenate([turned, jnp.zeros((OWN, OWN), jnp.float32)], axis=0)
    wide = jnp.concatenate([wide, jnp.zeros((W, W - OWN), jnp.float32)], axis=1)
    adj[0:OWN] = jnp.transpose(wide, (1, 0))[0:OWN]
    adj[OWN : 2 * OWN] = jnp.zeros((OWN, W), jnp.float32)
    adj[OWN + REST : OWN + 2 * REST] = adj[BIG:OWN]
    adj[OWN + 2 * REST : OWN + 3 * REST] = adj[0:REST]
    for _ in steps:
        pass


def weighted_half(half, other, own, got, vol, adj):
    span = pl.ds(pl.multiple_of(half * HALF, HALF), HALF)
    v = vol[0, span].astype(jnp.float32)
    hits = own[G, span].astype(jnp.float32) + got[G, span].astype(jnp.float32)
    factor = v / jnp.sqrt(1.0 + hits)
    total = own[0:G, span].astype(jnp.float32) + got[0:G, span].astype(jnp.float32)
    second = adj[pl.ds(pl.multiple_of(other, HALF), HALF)]
    rows = [total * factor[None], v[None], adj[span][None], second[None]]
    block = jnp.concatenate(rows, axis=0)
    return jnp.transpose(block, (1, 0, 2)).astype(jnp.bfloat16)


def source_b_kernel(own, got, vol, adj, b0):
    odd = lax.rem(lax.axis_index("dom"), 2)
    b0[...] = weighted_half(odd, (1 - odd) * HALF, own, got, vol, adj)


def source_a_kernel(own, got, vol, adj, b0, b1, a0, a1):
    odd = lax.rem(lax.axis_index("dom"), 2)
    half = weighted_half(1 - odd, OWN + (1 - odd) * HALF, own, got, vol, adj)
    b1[...] = half
    a0[pl.ds((1 - odd) * REST, HALF)] = half
    a0[pl.ds(odd * HALF, REST)] = b0[pl.ds((1 - odd) * REST, REST)]
    a1[...] = b0[pl.ds(odd * REST, REST)]


def neighbours(ref, row, lane):
    a = ref[:, row].astype(jnp.float32)
    return pltpu.roll(a, W - lane, 1) if lane else a


def make_lists(adj, lists):
    n = adj.shape[0]
    f32, bf16 = jnp.float32, jnp.bfloat16
    there = adj > 0.5
    ones = jnp.where(there, 1.0, 0.0)

    def triangle(m, strict):
        row = lax.broadcasted_iota(jnp.int32, (m, m), 0)
        col = lax.broadcasted_iota(jnp.int32, (m, m), 1)
        return jnp.where(col < row if strict else col <= row, 1.0, 0.0).astype(bf16)

    rank = jnp.dot(triangle(n, True), ones.astype(bf16), preferred_element_type=f32)
    rank = jnp.where(there, rank, -1.0)
    source = lax.broadcasted_iota(jnp.int32, (n, W), 0).astype(f32)
    code = source + 1.0 + 64.0 * (adj - 1.0)
    for r in range(n):
        picked = jnp.sum(jnp.where(rank == float(r), code, 0.0), axis=0, keepdims=True)
        lists[r : r + 1] = picked.astype(jnp.int32)
    terms = lax.dot_general(
        ones.astype(bf16), jnp.ones((n, W), bf16), (((0,), (0,)), ((), ())),
        preferred_element_type=f32,
    )[0:OWN]
    pairs = ((terms.astype(jnp.int32) + 1) >> 1).astype(f32)
    end = jnp.dot(triangle(OWN, False), pairs.astype(bf16), preferred_element_type=f32)
    lane = lax.broadcasted_iota(jnp.int32, (OWN, W), 1).astype(f32)
    for q in range(PAIR_ROWS):
        place = lane + float(q * W)
        past = end <= place
        target = jnp.sum(jnp.where(past, 1.0, 0.0), axis=0, keepdims=True)
        base = jnp.sum(jnp.where(past, pairs, 0.0), axis=0, keepdims=True)
        first = jnp.minimum(2.0 * (place[0:1] - base), float(n - 2))
        lists[n + q : n + q + 1] = (target + 256.0 * first).astype(jnp.int32)
    lists[n + PAIR_ROWS : n + PAIR_ROWS + 1] = end[OWN - 1 : OWN].astype(jnp.int32)


def list_rows(n):
    return n + 8


def add_terms(blocks, lists, tables, acc, mats, codes, sem):
    n = codes.shape[0] - 8
    copy = pltpu.make_async_copy(lists, codes, sem)
    copy.start()
    mats[0] = jnp.zeros((ROWS, W), jnp.bfloat16)
    at = 1
    for ref in blocks:
        mats[at : at + ref.shape[0]] = ref[...]
        at += ref.shape[0]
    copy.wait()

    def step(i, carry):
        for u in range(U):
            at = i * U + u
            entry = codes[n + (at >> 7), at & (W - 1)]
            x, r = entry & 255, entry >> 8
            two = [codes[r + j, x] for j in range(2)]
            term = jnp.dot(
                jnp.concatenate([mats[c & 63] for c in two], axis=1),
                jnp.concatenate([tables[c >> 6] for c in two], axis=0),
                preferred_element_type=jnp.float32,
            )
            acc[x] = acc[x] + term
        return carry

    lax.fori_loop(0, (codes[n + PAIR_ROWS, 0] + (U - 1)) >> 3, step, 0)


def own_kernel(first, second, tables, acc, lists, *scratch):
    adj = [neighbours(first, ADJ, OWN_LANE), neighbours(second, ADJ, OWN_LANE)]
    make_lists(jnp.concatenate(adj, axis=0), lists)

    def clear(i, carry):
        acc[i] = jnp.zeros((ROWS, W), jnp.float32)
        return carry

    lax.fori_loop(0, OWN + 1, clear, 0)
    add_terms((first, second), lists, tables, acc, *scratch)


def first_b_kernel(b0, tables, acc_in, acc, lists_b, lists, *scratch):
    if COPY_ALIASED:
        acc[...] = acc_in[...]
    make_lists(neighbours(b0, ADJ, 0), lists)
    make_lists(neighbours(b0, ADJ + 1, 0), lists_b)
    add_terms((b0,), lists, tables, acc, *scratch)


def first_a_kernel(a0, tables, acc_in, acc, lists_a, lists, *scratch):
    if COPY_ALIASED:
        acc[...] = acc_in[...]
    make_lists(neighbours(a0, ADJ, OWN), lists)
    make_lists(neighbours(a0, ADJ + 1, OWN)[REST : 2 * REST], lists_a)
    add_terms((a0,), lists, tables, acc, *scratch)


def finish(half, acc, out, stage, sems):
    copies = []
    for c in range(HALF // 8):
        first = pl.multiple_of(half * HALF + c * 8, 8)
        span = pl.ds(first, 8)
        scale = 1.0 / acc[span, G : G + 1]
        result = jnp.transpose(acc[span] * scale, (1, 0, 2))
        stage[c] = result[0:G].astype(jnp.bfloat16)
        copies.append(pltpu.make_async_copy(stage.at[c], out.at[0, :, span], sems.at[c]))
        copies[-1].start()
    for copy in copies:
        copy.wait()


def last_b_kernel(from_b, lists, tables, acc_in, out, acc, stage, sems, *scratch):
    if COPY_ALIASED:
        acc[...] = acc_in[...]
    add_terms((from_b,), lists, tables, acc, *scratch)
    finish(lax.rem(lax.axis_index("dom"), 2), acc, out, stage, sems)


def last_a_kernel(from_a, lists, tables, acc_in, out_in, out, acc, stage, sems, *scratch):
    if COPY_ALIASED:
        acc[...] = acc_in[...]
        pltpu.sync_copy(out_in, out)
    add_terms((from_a,), lists, tables, acc, *scratch)
    finish(1 - lax.rem(lax.axis_index("dom"), 2), acc, out, stage, sems)


def per_device(kernels, counts, volume, tables, pair_offset, pair_table):
    bf16, f32, i32 = jnp.bfloat16, jnp.float32, jnp.int32
    dma = pltpu.SemaphoreType.DMA
    kernels = in_hbm(jnp.transpose(kernels, (0, 1, 3, 2, 4)))
    counts = in_hbm(counts)
    pair_offset = jnp.transpose(pair_offset, (0, 1, 3, 2))
    pair_table = jnp.transpose(pair_table, (0, 1, 3, 2))
    sums = on_chip((G + 1, OWN, W), bf16)
    scratch = [
        pltpu.VMEM((2, G, OWN, W), bf16),
        pltpu.VMEM((2, OWN, W), i32),
        dma((len(PIECES),)),
        dma,
    ]

    to_other = pl.pallas_call(
        send_kernel,
        out_shape=sums,
        in_specs=[HBM, HBM],
        out_specs=VMEM,
        scratch_shapes=scratch,
        compiler_params=params(6),
        cost_estimate=cost(1 << 20, 4 << 20),
        name="send",
    )(kernels, counts)
    got = lax.ppermute(to_other, "event", [(0, 1), (1, 0)])
    own, adj = pl.pallas_call(
        keep_kernel,
        out_shape=[sums, on_chip((2 * OWN, W), f32)],
        in_specs=[HBM, HBM, VMEM, VMEM],
        out_specs=[VMEM, VMEM],
        scratch_shapes=scratch,
        compiler_params=params(6),
        cost_estimate=cost(1 << 20, 4 << 20),
        name="keep",
    )(kernels, counts, pair_offset, pair_table)

    def blocks(n):
        return on_chip((n, ROWS, W), bf16)

    count = lax.axis_size("dom")

    def swapped(value, start):
        pairs = [(a, a + 1) for a in range(start, count - 1, 2)]
        pairs = pairs + [(b, a) for a, b in pairs]
        return in_vmem(lax.ppermute(value, "dom", pairs))

    first = pl.pallas_call(
        source_b_kernel,
        out_shape=blocks(HALF),
        in_specs=[VMEM] * 4,
        out_specs=VMEM,
        compiler_params=params(6),
        cost_estimate=cost(1 << 20, 2 << 20),
        name="source_b",
    )(own, in_vmem(got), volume, adj)
    b0 = swapped(first, 1)
    second, to_a, rest = pl.pallas_call(
        source_a_kernel,
        out_shape=[blocks(HALF), blocks(BIG), blocks(REST)],
        in_specs=[VMEM] * 5,
        out_specs=[VMEM] * 3,
        compiler_params=params(6),
        cost_estimate=cost(1 << 20, 2 << 20),
        name="source_a",
    )(own, in_vmem(got), volume, adj, first)
    a0 = swapped(to_a, 0)
    b1 = swapped(second, 1)
    a1 = swapped(rest, 0)

    acc_shape = on_chip((OWN + 1, ROWS, W), f32)
    out_shape = jax.ShapeDtypeStruct((1, G, OWN, W), bf16)
    term = 2 * ROWS * W * W

    def lists(n):
        return (list_rows(n), W)

    def work(n):
        return [pltpu.VMEM((n + 1, ROWS, W), bf16), pltpu.SMEM(lists(n), i32), dma]

    stage = [pltpu.VMEM((HALF // 8, G, 8, W), bf16), dma((HALF // 8,))]
    acc = pl.pallas_call(
        own_kernel,
        out_shape=acc_shape,
        in_specs=[VMEM] * 3,
        out_specs=VMEM,
        scratch_shapes=[pltpu.VMEM(lists(OWN), i32)] + work(OWN),
        compiler_params=params(6),
        cost_estimate=cost(256 * term, 16 << 20),
        name="own_terms",
    )(first, second, tables)

    def first_terms(kernel, value, acc, n, second):
        return pl.pallas_call(
            kernel,
            out_shape=[acc_shape, on_chip(lists(second), i32)],
            in_specs=[VMEM] * 3,
            out_specs=[VMEM] * 2,
            scratch_shapes=[pltpu.VMEM(lists(n), i32)] + work(n),
            input_output_aliases={2: 0},
            compiler_params=params(6),
            cost_estimate=cost(96 * term, 6 << 20),
        )(value, tables, acc)

    acc, lists_b = first_terms(first_b_kernel, b0, acc, HALF, HALF)
    acc, lists_a = first_terms(first_a_kernel, a0, acc, BIG, REST)
    out, acc = pl.pallas_call(
        last_b_kernel,
        out_shape=[out_shape, acc_shape],
        in_specs=[VMEM] * 4,
        out_specs=[HBM, VMEM],
        scratch_shapes=stage + work(HALF),
        input_output_aliases={3: 1},
        compiler_params=params(6),
        cost_estimate=cost(32 * term, 2 << 20),
        name="last_b",
    )(b1, lists_b, tables, acc)
    out, _ = pl.pallas_call(
        last_a_kernel,
        out_shape=[out_shape, acc_shape],
        in_specs=[VMEM] * 4 + [HBM],
        out_specs=[HBM, VMEM],
        scratch_shapes=stage + work(REST),
        input_output_aliases={3: 1, 4: 0},
        compiler_params=params(6),
        cost_estimate=cost(32 * term, 2 << 20),
        name="last_a",
    )(a1, lists_a, tables, acc, out)
    return jnp.transpose(out, (0, 2, 1, 3))


def solution(mesh):
    in_specs = (
        P("event", "dom", None, None, None),
        P("event", "dom", None, None),
        P("dom", "event", None),
        P(),
        P("dom", "event", None, None),
        P("dom", "event", None, None),
    )
    return jax.shard_map(
        per_device,
        mesh=mesh,
        in_specs=in_specs,
        out_specs=P("dom", "event", None, None),
        check_vma=False,
    )
```

```python
import functools

import jax
import jax.numpy as jnp
from jax import lax
from jax.experimental import pallas as pl
from jax.experimental.pallas import tpu as pltpu
from jax.sharding import PartitionSpec as P


OWN = 32
HALF = OWN // 2
G = 125
ADJ = G + 1
ROWS = 128
W = 128
PB = 16
U = 8
PAIR_ROWS = 3
OWN_LANE = 2 * OWN
MIB = 1 << 20
COPY_ALIASED = False


HBM = pl.BlockSpec(memory_space=pltpu.HBM)
VMEM = pl.BlockSpec(memory_space=pltpu.VMEM)
SMEM = pl.BlockSpec(memory_space=pltpu.SMEM)


def on_chip(shape, dtype):
    return pltpu.VMEM(shape, dtype)


def in_vmem(x):
    return pltpu.with_memory_space_constraint(x, pltpu.VMEM)


def in_hbm(x):
    return pltpu.with_memory_space_constraint(x, pltpu.HBM)


def params(mib):
    return pltpu.CompilerParams(vmem_limit_bytes=mib * MIB)


def cost(flops, nbytes):
    return pl.CostEstimate(flops=flops, bytes_accessed=nbytes, transcendentals=0)


PIECES = tuple((first, min(16, G - first)) for first in range(0, G, 16))


def partial_sums(kern, counts, base, out, buf, cbuf, sems, csem):
    copies = []
    for n, (first, size) in enumerate(PIECES):
        span = pl.ds(first, size)
        copies.append(
            pltpu.make_async_copy(
                kern.at[:, 0, span, pl.ds(base, OWN)], buf.at[:, span], sems.at[n]
            )
        )
    ccopy = pltpu.make_async_copy(counts.at[:, 0, pl.ds(base, OWN)], cbuf, csem)
    for copy in copies + [ccopy]:
        copy.start()
    yield
    for copy, (first, size) in zip(copies, PIECES):
        copy.wait()
        span = slice(first, first + size)
        total = buf[0, span].astype(jnp.float32) + buf[1, span].astype(jnp.float32)
        out[span] = total.astype(jnp.bfloat16)
    ccopy.wait()
    out[G] = (cbuf[0] + cbuf[1]).astype(jnp.float32).astype(jnp.bfloat16)


def send_kernel(kern, counts, out, *scratch):
    base = (1 - lax.axis_index("event")) * OWN
    for _ in partial_sums(kern, counts, base, out, *scratch):
        pass


def keep_kernel(kern, counts, off, tab, out, adj, *scratch):
    steps = partial_sums(kern, counts, lax.axis_index("event") * OWN, out, *scratch)
    next(steps)
    odd = lax.rem(lax.axis_index("dom"), 2)
    b = lax.broadcasted_iota(jnp.int32, (PB, OWN), 1)
    x = off[0, 0] + b
    part = x >> 5
    group = jnp.where(part == 1, 2, jnp.where(part == 0, odd, 1 - odd))
    lane = (x & (OWN - 1)) + group * OWN
    value = (tab[0, 0] + 1).astype(jnp.float32)
    spot = lax.broadcasted_iota(jnp.int32, (3 * OWN, OWN), 0)
    turned = jnp.zeros((3 * OWN, OWN), jnp.float32)
    for k in range(PB):
        turned = turned + jnp.where(spot == lane[k : k + 1], value[k : k + 1], 0.0)
    wide = jnp.concatenate([turned, jnp.zeros((OWN, OWN), jnp.float32)], axis=0)
    wide = jnp.concatenate([wide, jnp.zeros((W, W - OWN), jnp.float32)], axis=1)
    adj[...] = jnp.transpose(wide, (1, 0))[0:OWN]
    for _ in steps:
        pass


def source_kernel(leaves_first, own, got, vol, adj, dst):
    odd = lax.rem(lax.axis_index("dom"), 2)
    half = odd if leaves_first else 1 - odd
    span = pl.ds(pl.multiple_of(half * HALF, HALF), HALF)
    rest = pl.ds(pl.multiple_of((1 - half) * HALF, HALF), HALF)
    v = vol[0, span].astype(jnp.float32)
    hits = own[G, span].astype(jnp.float32) + got[G, span].astype(jnp.float32)
    factor = v / jnp.sqrt(1.0 + hits)
    total = own[0:G, span].astype(jnp.float32) + got[0:G, span].astype(jnp.float32)
    rows = [total * factor[None], v[None], adj[span][None], adj[rest][None]]
    block = jnp.concatenate(rows, axis=0)
    dst[...] = jnp.transpose(block, (1, 0, 2)).astype(jnp.bfloat16)


def neighbours(ref, row, lane):
    a = ref[:, row].astype(jnp.float32)
    return pltpu.roll(a, W - lane, 1) if lane else a


def make_lists(adj, lists):
    n = adj.shape[0]
    f32, bf16 = jnp.float32, jnp.bfloat16
    there = adj > 0.5
    ones = jnp.where(there, 1.0, 0.0)

    def triangle(m, strict):
        row = lax.broadcasted_iota(jnp.int32, (m, m), 0)
        col = lax.broadcasted_iota(jnp.int32, (m, m), 1)
        return jnp.where(col < row if strict else col <= row, 1.0, 0.0).astype(bf16)

    rank = jnp.dot(triangle(n, True), ones.astype(bf16), preferred_element_type=f32)
    rank = jnp.where(there, rank, -1.0)
    source = lax.broadcasted_iota(jnp.int32, (n, W), 0).astype(f32)
    code = source + 1.0 + 64.0 * (adj - 1.0)
    for r in range(n):
        picked = jnp.sum(jnp.where(rank == float(r), code, 0.0), axis=0, keepdims=True)
        lists[r : r + 1] = picked.astype(jnp.int32)
    terms = lax.dot_general(
        ones.astype(bf16), jnp.ones((n, W), bf16), (((0,), (0,)), ((), ())),
        preferred_element_type=f32,
    )[0:OWN]
    pairs = ((terms.astype(jnp.int32) + 1) >> 1).astype(f32)
    end = jnp.dot(triangle(OWN, False), pairs.astype(bf16), preferred_element_type=f32)
    lane = lax.broadcasted_iota(jnp.int32, (OWN, W), 1).astype(f32)
    for q in range(PAIR_ROWS):
        place = lane + float(q * W)
        past = end <= place
        target = jnp.sum(jnp.where(past, 1.0, 0.0), axis=0, keepdims=True)
        base = jnp.sum(jnp.where(past, pairs, 0.0), axis=0, keepdims=True)
        first = jnp.minimum(2.0 * (place[0:1] - base), float(n - 2))
        lists[n + q : n + q + 1] = (target + 256.0 * first).astype(jnp.int32)
    lists[n + PAIR_ROWS : n + PAIR_ROWS + 1] = end[OWN - 1 : OWN].astype(jnp.int32)


def list_rows(n):
    return n + 8


def add_terms(blocks, lists, tables, acc, mats, codes, sem, meanwhile=None):
    n = HALF * len(blocks)
    copy = pltpu.make_async_copy(lists, codes, sem)
    copy.start()
    mats[0] = jnp.zeros((ROWS, W), jnp.bfloat16)
    for i, ref in enumerate(blocks):
        mats[1 + i * HALF : 1 + (i + 1) * HALF] = ref[...]
    if meanwhile is not None:
        meanwhile()
    copy.wait()

    def step(i, carry):
        for u in range(U):
            at = i * U + u
            entry = codes[n + (at >> 7), at & (W - 1)]
            x, r = entry & 255, entry >> 8
            two = [codes[r + j, x] for j in range(2)]
            term = jnp.dot(
                jnp.concatenate([mats[c & 63] for c in two], axis=1),
                jnp.concatenate([tables[c >> 6] for c in two], axis=0),
                preferred_element_type=jnp.float32,
            )
            acc[x] = acc[x] + term
        return carry

    lax.fori_loop(0, (codes[n + PAIR_ROWS, 0] + (U - 1)) >> 3, step, 0)


def own_kernel(first, second, tables, acc, lists, *scratch):
    adj = [neighbours(first, ADJ, OWN_LANE), neighbours(second, ADJ, OWN_LANE)]
    make_lists(jnp.concatenate(adj, axis=0), lists)

    def clear(i, carry):
        acc[i] = jnp.zeros((ROWS, W), jnp.float32)
        return carry

    lax.fori_loop(0, OWN + 1, clear, 0)
    add_terms((first, second), lists, tables, acc, *scratch)


def chunk_kernel(from_b, from_a, tables, acc_in, acc, lists_a, lists_b, lists, *scratch):
    if COPY_ALIASED:
        acc[...] = acc_in[...]
    adj = [neighbours(from_b, ADJ, 0), neighbours(from_a, ADJ, OWN)]
    make_lists(jnp.concatenate(adj, axis=0), lists)
    make_lists(neighbours(from_a, ADJ + 1, OWN), lists_a)
    make_lists(neighbours(from_b, ADJ + 1, 0), lists_b)
    add_terms((from_b, from_a), lists, tables, acc, *scratch)


def finish(half, acc, out, stage, sems):
    copies = []
    for c in range(HALF // 8):
        first = pl.multiple_of(half * HALF + c * 8, 8)
        span = pl.ds(first, 8)
        scale = 1.0 / acc[span, G : G + 1]
        result = jnp.transpose(acc[span] * scale, (1, 0, 2))
        stage[c] = result[0:G].astype(jnp.bfloat16)
        copies.append(pltpu.make_async_copy(stage.at[c], out.at[0, :, span], sems.at[c]))
        copies[-1].start()
    return copies


def last_b_kernel(from_b, lists, tables, acc_in, acc, *scratch):
    if COPY_ALIASED:
        acc[...] = acc_in[...]
    add_terms((from_b,), lists, tables, acc, *scratch)


def last_a_kernel(from_a, lists, tables, acc_in, out, acc, stage, sems, *scratch):
    if COPY_ALIASED:
        acc[...] = acc_in[...]
    odd = lax.rem(lax.axis_index("dom"), 2)
    copies = []

    def finish_b():
        copies.extend(finish(odd, acc, out, stage.at[0], sems.at[0]))

    add_terms((from_a,), lists, tables, acc, *scratch, meanwhile=finish_b)
    copies.extend(finish(1 - odd, acc, out, stage.at[1], sems.at[1]))
    for copy in copies:
        copy.wait()


def per_device(kernels, counts, volume, tables, pair_offset, pair_table):
    bf16, f32, i32 = jnp.bfloat16, jnp.float32, jnp.int32
    dma = pltpu.SemaphoreType.DMA
    kernels = in_hbm(jnp.transpose(kernels, (0, 1, 3, 2, 4)))
    counts = in_hbm(counts)
    pair_offset = jnp.transpose(pair_offset, (0, 1, 3, 2))
    pair_table = jnp.transpose(pair_table, (0, 1, 3, 2))
    sums = on_chip((G + 1, OWN, W), bf16)
    scratch = [
        pltpu.VMEM((2, G, OWN, W), bf16),
        pltpu.VMEM((2, OWN, W), i32),
        dma((len(PIECES),)),
        dma,
    ]

    to_other = pl.pallas_call(
        send_kernel,
        out_shape=sums,
        in_specs=[HBM, HBM],
        out_specs=VMEM,
        scratch_shapes=scratch,
        compiler_params=params(6),
        cost_estimate=cost(1 << 20, 4 << 20),
        name="send",
    )(kernels, counts)
    got = lax.ppermute(to_other, "event", [(0, 1), (1, 0)])
    own, adj = pl.pallas_call(
        keep_kernel,
        out_shape=[sums, on_chip((OWN, W), f32)],
        in_specs=[HBM, HBM, VMEM, VMEM],
        out_specs=[VMEM, VMEM],
        scratch_shapes=scratch,
        compiler_params=params(6),
        cost_estimate=cost(1 << 20, 4 << 20),
        name="keep",
    )(kernels, counts, pair_offset, pair_table)

    def source(leaves_first):
        return pl.pallas_call(
            functools.partial(source_kernel, leaves_first),
            out_shape=on_chip((HALF, ROWS, W), bf16),
            in_specs=[VMEM] * 4,
            out_specs=VMEM,
            compiler_params=params(6),
            cost_estimate=cost(1 << 20, 2 << 20),
        )(own, in_vmem(got), volume, adj)

    count = lax.axis_size("dom")

    def swapped(value, start):
        pairs = [(a, a + 1) for a in range(start, count - 1, 2)]
        pairs = pairs + [(b, a) for a, b in pairs]
        return in_vmem(lax.ppermute(value, "dom", pairs))

    first = source(True)
    b0 = swapped(first, 1)
    second = source(False)
    a0 = swapped(second, 0)
    b1 = swapped(second, 1)
    a1 = swapped(first, 0)

    acc_shape = on_chip((OWN + 1, ROWS, W), f32)
    out_shape = jax.ShapeDtypeStruct((1, G, OWN, W), bf16)
    term = 2 * ROWS * W * W

    def lists(n):
        return (list_rows(n), W)

    def work(n):
        return [pltpu.VMEM((n + 1, ROWS, W), bf16), pltpu.SMEM(lists(n), i32), dma]

    stage = [pltpu.VMEM((2, HALF // 8, G, 8, W), bf16), dma((2, HALF // 8))]
    acc = pl.pallas_call(
        own_kernel,
        out_shape=acc_shape,
        in_specs=[VMEM] * 3,
        out_specs=VMEM,
        scratch_shapes=[pltpu.VMEM(lists(OWN), i32)] + work(OWN),
        compiler_params=params(6),
        cost_estimate=cost(256 * term, 16 << 20),
        name="own_terms",
    )(first, second, tables)
    acc, lists_a, lists_b = pl.pallas_call(
        chunk_kernel,
        out_shape=[acc_shape] + [on_chip(lists(HALF), i32)] * 2,
        in_specs=[VMEM] * 4,
        out_specs=[VMEM] * 3,
        scratch_shapes=[pltpu.VMEM(lists(OWN), i32)] + work(OWN),
        input_output_aliases={3: 0},
        compiler_params=params(6),
        cost_estimate=cost(192 * term, 12 << 20),
        name="chunk_terms",
    )(b0, a0, tables, acc)
    acc = pl.pallas_call(
        last_b_kernel,
        out_shape=acc_shape,
        in_specs=[VMEM] * 4,
        out_specs=VMEM,
        scratch_shapes=work(HALF),
        input_output_aliases={3: 0},
        compiler_params=params(6),
        cost_estimate=cost(32 * term, 2 << 20),
        name="last_b",
    )(b1, lists_b, tables, acc)
    out, _ = pl.pallas_call(
        last_a_kernel,
        out_shape=[out_shape, acc_shape],
        in_specs=[VMEM] * 4,
        out_specs=[HBM, VMEM],
        scratch_shapes=stage + work(HALF),
        input_output_aliases={3: 1},
        compiler_params=params(6),
        cost_estimate=cost(32 * term, 2 << 20),
        name="last_a",
    )(a1, lists_a, tables, acc)
    return jnp.transpose(out, (0, 2, 1, 3))


def solution(mesh):
    in_specs = (
        P("event", "dom", None, None, None),
        P("event", "dom", None, None),
        P("dom", "event", None),
        P(),
        P("dom", "event", None, None),
        P("dom", "event", None, None),
    )
    return jax.shard_map(
        per_device,
        mesh=mesh,
        in_specs=in_specs,
        out_specs=P("dom", "event", None, None),
        check_vma=False,
    )
```
